32 devices in a mesh: cell: 2 (over y), gene: 16 (over z, x, core).
Axes of the slice: x: 2, y: 2, z: 4, core: 2. Of those that a mesh axis runs over, the one named last changes fastest.
Arguments:
- blocks: bfloat16 [1536, 256, 256], P(('cell', 'gene')), may hold values from 0 to 255, as said below
- block_rows: int32 [1536], P(('cell', 'gene')), may hold values from 0 to 15, as said below
- block_cols: int32 [1536], P(('cell', 'gene')), may hold values from 0 to 3, as said below
- block_count: int32 [32], P(('cell', 'gene')), may hold values from 2 to 48, as said below
- cell_factor: float32 [8192, 128], P(('cell', 'gene')), as said below
- gene_factor: float32 [16384, 128], P('gene'), as said below
Outputs:
- cell_new: float32 [8192, 128], P(('cell', 'gene'))
- gene_new: float32 [16384, 128], P('gene')
The draws below stay inside these ranges and needn't reach their ends.
Inputs may be any that keep to these rules, and one draw needn't show every extreme that they name: `blocks`: counts are whole numbers. `block_rows`: within one device the live slots and the padding slots name distinct block positions. `block_cols`: within one device the live slots and the padding slots name distinct block positions. `block_count`: some device has all 48 slots live. `cell_factor`: positive entries. `gene_factor`: positive entries.
All inputs are finite; a program needn't handle non-finite values.
Results may differ from the reference program's by a relative error of at most 0.00084.
Values may be sent and summed in bfloat16 or wider, within the bound.
A program may use at most 64 MiB of HBM per device.

```python
import jax
import jax.numpy as jnp
from jax import lax

BLK = 256
R = 128
GENE_DEV = 1024
CELL_DEV = 4096
NB_DEV = 48
CELLS = 8192
GENES = 16384
N_CELL = 2
N_GENE = 16


def positions(key):
    devs = N_CELL * N_GENE
    keys = jax.random.split(jax.random.fold_in(key, 7), devs)
    total = CELL_DEV // BLK * (GENE_DEV // BLK)
    picked = jax.vmap(lambda one: jax.random.permutation(one, total)[:NB_DEV])(keys)
    return picked.reshape(-1).astype(jnp.int32)


def draw_block_rows(key, part):
    return (positions(key) // (GENE_DEV // BLK)).astype(jnp.int32)


def draw_block_cols(key, part):
    return (positions(key) % (GENE_DEV // BLK)).astype(jnp.int32)


def draw_block_count(key, part):
    devs = N_CELL * N_GENE
    first_key = jax.random.fold_in(key, 21)
    second_key = jax.random.fold_in(key, 22)
    third_key = jax.random.fold_in(key, 23)
    left = jax.random.randint(first_key, (devs,), 0, NB_DEV - 1)
    right = jax.random.randint(second_key, (devs,), 0, NB_DEV - 1)
    counts = 2 + left * right // (NB_DEV - 2)
    fullest = jax.random.randint(third_key, (), 0, devs)
    return jnp.where(jnp.arange(devs) == fullest, NB_DEV, counts).astype(jnp.int32)


def draw_blocks(key, part):
    shape = (N_CELL * N_GENE * NB_DEV, BLK, BLK)
    inner = jax.random.fold_in(key, 3)
    values = jax.random.randint(inner, shape, 0, 256)
    return values.astype(jnp.float32).astype(jnp.bfloat16)


def factor_draw(key, count):
    base_key = jax.random.fold_in(key, 41)
    rank_key = jax.random.fold_in(key, 42)
    boost_key = jax.random.fold_in(key, 43)
    rising = 1.0 + 2.0 * jnp.arange(count, dtype=jnp.float32)[:, None] / count
    leading = max(1, R // 32)
    chosen_ranks = jax.random.randint(rank_key, (count, leading), 0, R)
    ranks = jnp.arange(R, dtype=jnp.int32)[None, :]
    marked = jnp.zeros((count, R), jnp.float32)
    for which in range(leading):
        marked = jnp.maximum(marked, (chosen_ranks[:, which:which + 1] == ranks).astype(jnp.float32))
    base = jnp.exp(jax.random.uniform(base_key, (count, R), jnp.float32, jnp.log(0.05), jnp.log(0.5)))
    boost = jnp.exp(jax.random.uniform(boost_key, (count, R), jnp.float32, jnp.log(3.0), jnp.log(12.0)))
    entries = jnp.where(marked > 0.0, boost, base)
    return (entries * rising).astype(jnp.float32)


def draw_cell_factor(key, part):
    return factor_draw(jax.random.fold_in(key, 51), CELLS)


def draw_gene_factor(key, part):
    return factor_draw(jax.random.fold_in(key, 52), GENES)


def setup_inputs(seed: int = 0) -> dict:
    arg_keys = jax.random.split(jax.random.key(seed), 7)
    blocks = draw_blocks(jax.random.fold_in(arg_keys[6], 71), 0)
    block_rows = draw_block_rows(jax.random.fold_in(arg_keys[6], 71), 0)
    block_cols = draw_block_cols(jax.random.fold_in(arg_keys[6], 71), 0)
    block_count = draw_block_count(jax.random.fold_in(arg_keys[6], 71), 0)
    cell_factor = draw_cell_factor(jax.random.fold_in(arg_keys[6], 71), 0)
    gene_factor = draw_gene_factor(jax.random.fold_in(arg_keys[6], 71), 0)
    return dict(blocks=blocks, block_rows=block_rows, block_cols=block_cols, block_count=block_count, cell_factor=cell_factor, gene_factor=gene_factor)


def block_ratio(tiles, row_tiles, col_tiles, live):
    model = jnp.einsum('nir,njr->nij', row_tiles.astype(jnp.float32), col_tiles.astype(jnp.float32))
    return (tiles.astype(jnp.float32) / model * live[:, None, None]).astype(jnp.bfloat16)


def reference(blocks, block_rows, block_cols, block_count, cell_factor, gene_factor):
    devs = N_CELL * N_GENE
    row_blocks = CELL_DEV // BLK
    col_blocks = GENE_DEV // BLK
    tiles = blocks.reshape(devs, NB_DEV, BLK, BLK)
    rows = block_rows.reshape(devs, NB_DEV).astype(jnp.int32)
    cols = block_cols.reshape(devs, NB_DEV).astype(jnp.int32)
    counts = block_count.astype(jnp.int32)
    order = jnp.arange(devs, dtype=jnp.int32)
    cell_bf = cell_factor.astype(jnp.bfloat16)
    gene_bf = gene_factor.astype(jnp.bfloat16)

    def prepare(cell_src, item):
        tile, row, col, count, index = item
        cstart = ((index // N_GENE) * CELL_DEV).astype(jnp.int32)
        gstart = ((index % N_GENE) * GENE_DEV).astype(jnp.int32)
        w_tile = lax.dynamic_slice_in_dim(cell_src, cstart, CELL_DEV, 0)
        h_tile = lax.dynamic_slice_in_dim(gene_bf, gstart, GENE_DEV, 0)
        live = (jnp.arange(NB_DEV, dtype=jnp.int32) < count).astype(jnp.float32)
        row_tiles = w_tile.reshape(row_blocks, BLK, R)[row]
        col_tiles = h_tile.reshape(col_blocks, BLK, R)[col]
        ratio = block_ratio(tile, row_tiles, col_tiles, live)
        return ratio, row_tiles, col_tiles, cstart, gstart

    def first(carry, item):
        ratio, row_tiles, col_tiles, cstart, gstart = prepare(cell_bf, item)
        terms = jnp.einsum('nij,njr->nir', ratio.astype(jnp.float32), col_tiles.astype(jnp.float32))
        sums = jax.ops.segment_sum(terms, item[1], num_segments=row_blocks).reshape(CELL_DEV, R)
        old = lax.dynamic_slice_in_dim(carry, cstart, CELL_DEV, 0)
        return lax.dynamic_update_slice_in_dim(carry, old + sums, cstart, 0), None

    numer_w, unused = lax.scan(first, jnp.zeros((CELLS, R), jnp.float32), (tiles, rows, cols, counts, order))
    gene_sums = jnp.sum(gene_factor, 0)
    cell_new = cell_factor * numer_w / gene_sums
    new_bf = cell_new.astype(jnp.bfloat16)

    def second(carry, item):
        ratio, row_tiles, col_tiles, cstart, gstart = prepare(new_bf, item)
        terms = jnp.einsum('nij,nir->njr', ratio.astype(jnp.float32), row_tiles.astype(jnp.float32))
        sums = jax.ops.segment_sum(terms, item[2], num_segments=col_blocks).reshape(GENE_DEV, R)
        old = lax.dynamic_slice_in_dim(carry, gstart, GENE_DEV, 0)
        return lax.dynamic_update_slice_in_dim(carry, old + sums, gstart, 0), None

    numer_h, unused = lax.scan(second, jnp.zeros((GENES, R), jnp.float32), (tiles, rows, cols, counts, order))
    cell_sums = jnp.sum(cell_new, 0)
    gene_new = gene_factor * numer_h / cell_sums
    return cell_new, gene_new
```

```python
import functools

import jax
import jax.numpy as jnp
from jax import lax
from jax.experimental import pallas as pl
from jax.experimental.pallas import tpu as pltpu
from jax.sharding import PartitionSpec as P

MESH = pl.DeviceIdType.MESH
F32 = jnp.float32
BF = jnp.bfloat16
I16 = jnp.int16
I32 = jnp.int32
CORES = 2
FAR = 4
PARTS = 2
LAST = 3


def digits(group):
    return FAR, group // (FAR * CORES), CORES


def flip(v, k, n):
    if k == 0:
        return v
    if k == n - 1:
        return n - 1 - v
    if k == n // 2:
        return lax.rem(v + n // 2, n)
    return v + 1 - 2 * lax.rem(v, 2)


class Spot:
    def __init__(self, group):
        self.group = group
        self.far, self.near, self.cores = digits(group)
        self.me = lax.axis_index("gene")
        self.a = self.me // (self.near * self.cores)
        self.b = lax.rem(self.me // self.cores, self.near)
        self.c = lax.rem(self.me, self.cores)

    def unit(self, k, e):
        return flip(self.a, k, self.far) * self.near + flip(self.b, e, self.near)

    def peer(self, k, e, core):
        return {"gene": self.unit(k, e) * self.cores + core}


def send(src, dst, send_sem, recv_sem, where):
    copy = pltpu.make_async_remote_copy(
        src_ref=src, dst_ref=dst, send_sem=send_sem, recv_sem=recv_sem,
        device_id=where, device_id_type=MESH,
    )
    copy.start()
    return copy


def greet(axis, size):
    barrier = pltpu.get_barrier_semaphore()
    me = lax.axis_index(axis)
    for d in range(1, size):
        pl.semaphore_signal(
            barrier, inc=1, device_id={axis: lax.rem(me + d, size)}, device_id_type=MESH
        )


def encode(value, code, scale):
    top = jnp.max(jnp.abs(value), axis=0, keepdims=True)
    factor = jnp.where(top > 0.0, 32767.0 / top, 0.0)
    code[...] = jnp.round(value * factor).astype(jnp.int32).astype(jnp.int16)
    scale[...] = top * (1.0 / 32767.0)


def decode(code, scale):
    return code[...].astype(jnp.int32).astype(F32) * scale[...]


class Gather:
    def __init__(self, spot, out, prow, sems):
        self.spot, self.out, self.prow = spot, out, prow
        self.zs, self.zr, self.xs, self.xr, self.cs, self.cr = sems
        self.zc, self.xc, self.cc = {}, {}, {}

    def place(self, h, k, e):
        spot = self.spot
        first = pl.multiple_of(spot.c * self.prow, self.prow)
        return self.out.at[h, spot.unit(k, e), pl.ds(first, self.prow)]

    def start(self, h):
        spot, src = self.spot, self.place(h, 0, 0)
        for k in range(1, spot.far):
            self.zc[h, k] = send(src, src, self.zs.at[h, k], self.zr.at[h, k],
                                 spot.peer(k, 0, spot.c))
        self.forward(h, 0)

    def forward(self, h, k):
        spot, src = self.spot, self.place(h, k, 0)
        for e in range(1, spot.near):
            self.xc[h, k, e] = send(src, src, self.xs.at[h, k, e], self.xr.at[h, k, e],
                                    spot.peer(0, e, spot.c))
        self.pair(h, k, 0)

    def pair(self, h, k, e):
        spot, src = self.spot, self.place(h, k, e)
        self.cc[h, k, e] = send(src, src, self.cs.at[h, k, e], self.cr.at[h, k, e],
                                spot.peer(0, 0, 1 - spot.c))

    def take_far(self, h, k):
        self.zc[h, k].wait_recv()
        self.forward(h, k)

    def take_near(self, h, k, e):
        self.xc[h, k, e].wait_recv()
        self.pair(h, k, e)

    def ready(self, h, k, e):
        self.cc[h, k, e].wait_recv()

    def copies(self):
        return [*self.zc.values(), *self.xc.values(), *self.cc.values()]


def gather_sems(far, near):
    dma = pltpu.SemaphoreType.DMA
    return [dma((PARTS, far))] * 2 + [dma((PARTS, far, near))] * 4


class Plan:
    def __init__(self, far, near):
        self.far, self.near = far, near
        self.time = 0.0
        self.free = {"c": 0.0, "x": 0.0, "z": 0.0}
        self.arrive = {}
        self.done = {}
        self.order = []

    def post(self, link, key, extra=0.0, weight=1.0):
        wire = {"c": 0.1, "x": 1.4, "z": 1.4}[link] / PARTS * weight
        wait = {"c": 0.9, "x": 1.9, "z": 1.9}[link]
        self.free[link] = max(self.free[link], self.time) + wire
        self.arrive[key] = self.free[link] + wait + extra

    def begin(self, name, h):
        for k in range(1, self.far):
            self.post("z", (name, "z", h, k), 0.7 * (k - 1), 2.0 if k == 3 else 1.0)
        self.ahead(name, h, 0)

    def ahead(self, name, h, k):
        for e in range(1, self.near):
            self.post("x", (name, "x", h, k, e))
        self.post("c", (name, "c", h, k, 0))

    def tasks(self):
        far, near = range(self.far), range(self.near)
        out = []
        for h in range(PARTS):
            for name in ("one", "two"):
                for k in far[1:]:
                    out.append(((name, "far", h, k), [(name, "z", h, k)], 0.02))
                for k in far:
                    for e in near[1:]:
                        out.append(((name, "near", h, k, e), [(name, "x", h, k, e)], 0.02))
            need = [("p1", h, 0, 0)] + [("p2", h, 0, e) for e in near[1:]]
            out.append((("fresh", h), need + [("p3", h, k) for k in far[1:]], 0.4))
            for k in far[1:]:
                need = [("p1", h, k, 0)] + [("p2", h, k, e) for e in near[1:]]
                out.append((("sum", h, k), need, 0.25))
            for k in far:
                for e in near[1:]:
                    out.append((("mix", h, k, e), [("p1", h, k, e)], 0.2))
        spread = [(h, k, e) for h in range(PARTS) for e in reversed(near) for k in [*far[1:], 0]]
        out += [(("first", *u), [("one", "c", *u)], 1.24 / PARTS * (self.near / 2) ** 0) for u in spread]
        out += [(("second", *u), [("two", "c", *u)], 1.24 / PARTS) for u in spread]
        return out

    def run(self, task):
        kind = task[0]
        if kind == "first":
            self.post("c", ("p1", *task[1:]))
        elif kind == "mix":
            self.post("x", ("p2", *task[1:]))
        elif kind == "sum":
            self.post("z", ("p3", *task[1:]), 0.7 * (task[2] - 1), 2.0 if task[2] == 3 else 1.0)
        elif kind == "fresh":
            self.begin("two", task[1])
        elif kind in ("one", "two") and task[1] == "far":
            self.ahead(kind, task[2], task[3])
        elif kind in ("one", "two"):
            self.post("c", (kind, "c", *task[2:]))

    def build(self):
        for h in range(PARTS):
            self.begin("one", h)
        left = self.tasks()
        while left:
            known = [(max(self.arrive[n] for n in need), i) for i, (_, need, _) in enumerate(left)
                     if all(n in self.arrive for n in need)]
            ready = [i for when, i in known if when <= self.time]
            if not ready:
                self.time = min(when for when, _ in known)
                continue
            task, _, cost = left.pop(min(ready))
            self.time += cost
            self.run(task)
            self.order.append(task)
        return self.order


def step_kernel(group, cells, blocks, brow, bcol, bcount, cell_in, gene_in, cell_new, gene_new,
                held, spread, table, cell, gene, gene_bf, flipped, own_sum, parts, cell_bf,
                next_sum, next_parts, next_cell, numer, p1, p2, p3, t2, t3,
                p2m, p3m, t2m, t3m, acc, code, codem, other, otherm, group_sum, other_sum, *sems):
    spot = Spot(group)
    far, near, cores = spot.far, spot.near, spot.cores
    c = spot.c
    slots, width, _ = blocks.shape
    tiles = gene.shape[0]
    rows = cell.shape[0]
    prow = rows // PARTS
    sub = width // rows
    one_sems, two_sems = sems[0:6], sems[6:12]
    s1, r1, s2, r2, s3, r3, gs, gr, ns, nr, fs, fr, os, orr, ls, u2, v2, u3, v3, uf, vf = sems[12:]
    greet("gene", group)
    greet("cell", cells)
    load_cell = pltpu.make_async_copy(cell_in, cell, ls.at[0])
    load_cell.start()
    load_gene = pltpu.make_async_copy(gene_in, gene, ls.at[1])
    load_gene.start()
    load = pltpu.make_async_copy(blocks, held.at[pl.ds(0, slots)], ls.at[2])
    load.start()

    lane = lax.broadcasted_iota(I32, (1, slots), 1)
    where = jnp.where(lane < bcount[0], brow[...] * tiles + bcol[...], -1)
    at = lax.broadcasted_iota(I32, (spread.shape[0], slots), 0)
    found = jnp.min(jnp.where(at == where, lane, slots), axis=1, keepdims=True)
    spread[...] = jnp.broadcast_to(found, spread.shape)
    load_table = pltpu.make_async_copy(spread, table, ls.at[3])
    load_table.start()
    held[slots] = jnp.zeros((width, width), BF)

    one = Gather(spot, cell_bf, prow, one_sems)
    two = Gather(spot, next_cell, prow, two_sems)
    load_cell.wait()
    for h in range(PARTS):
        one.place(h, 0, 0)[...] = cell[pl.ds(h * prow, prow), :].astype(BF)
    pl.semaphore_wait(pltpu.get_barrier_semaphore(), group - 1 + cells - 1)
    for h in range(PARTS):
        one.start(h)

    def share(src, out, ss, sr):
        return [
            send(src, out.at[spot.me], ss.at[d], sr.at[d], {"gene": lax.rem(spot.me + d, group)})
            for d in range(1, group)
        ]

    load_gene.wait()
    first_sum = jnp.zeros((1, gene.shape[-1]), F32)
    for j in range(tiles):
        first_sum += jnp.sum(gene[j], axis=0, keepdims=True)
    own_sum[...] = first_sum
    parts[spot.me] = first_sum
    shared = share(own_sum, parts, gs, gr)
    for j in range(tiles):
        gene_bf[j] = gene[j].astype(BF)
        flipped[j] = gene[j].astype(BF).T
    acc[...] = jnp.zeros_like(acc)
    load_table.wait()
    load.wait()

    def ratio_of(source, h, u, j):
        rows_bf = source[h, u]
        found = []
        for core in range(cores):
            g = u * cores + core
            slot = table[(g // sub) * tiles + j, 0]
            if sub == 1:
                found.append(held[slot, pl.ds(h * prow, prow), :])
            else:
                first = pl.multiple_of(lax.rem(g, sub) * rows + h * prow, prow)
                found.append(held[slot, pl.ds(first, prow), :])
        x = jnp.concatenate(found, axis=0)
        model = jnp.dot(rows_bf, flipped[j], preferred_element_type=F32)
        return (x.astype(F32) / model).astype(BF), rows_bf

    c1, c2, c3 = {}, {}, {}
    mine_at = pl.ds(pl.multiple_of(c * prow, prow), prow)
    theirs_at = pl.ds(pl.multiple_of((1 - c) * prow, prow), prow)

    def first(h, k, e):
        one.ready(h, k, e)
        u = spot.unit(k, e)
        total = None
        for j in range(tiles):
            ratio, _ = ratio_of(cell_bf, h, u, j)
            term = jnp.dot(ratio, gene_bf[j], preferred_element_type=F32)
            total = term if total is None else total + term
        numer[h, u] = total
        c1[h, k, e] = send(numer.at[h, u, theirs_at], p1.at[h, k, e], s1.at[h, k, e],
                           r1.at[h, k, e], spot.peer(0, 0, 1 - c))

    def weight(h, u):
        return jnp.mean(cell_bf[h, u, mine_at].astype(F32), axis=1, keepdims=True)

    def both(h, k, e):
        c1[h, k, e].wait_recv()
        u = spot.unit(k, e)
        return (numer[h, u, mine_at] + p1[h, k, e]) * weight(h, u)

    def mix(h, k, e):
        encode(both(h, k, e), t2.at[h, k, e], t2m.at[h, k, e])
        where = spot.peer(0, e, c)
        c2[h, k, e] = (
            send(t2.at[h, k, e], p2.at[h, k, e], s2.at[h, k, e], r2.at[h, k, e], where),
            send(t2m.at[h, k, e], p2m.at[h, k, e], u2.at[h, k, e], v2.at[h, k, e], where),
        )

    def summed(h, k):
        value = both(h, k, 0)
        for e in range(1, near):
            for copy in c2[h, k, e]:
                copy.wait_recv()
            value += decode(p2.at[h, k, e], p2m.at[h, k, e])
        return value

    def stage_sum(h, k):
        encode(summed(h, k), t3.at[h, k], t3m.at[h, k])
        where = spot.peer(k, 0, c)
        c3[h, k] = (
            send(t3.at[h, k], p3.at[h, k], s3.at[h, k], r3.at[h, k], where),
            send(t3m.at[h, k], p3m.at[h, k], u3.at[h, k], v3.at[h, k], where),
        )

    sums_of = {}

    def fresh(h):
        if "total" not in sums_of:
            for copy in shared:
                copy.wait()
            sums_of["total"] = jnp.sum(parts[...], axis=0)
        value = summed(h, 0)
        for k in range(1, far):
            for copy in c3[h, k]:
                copy.wait_recv()
            value += decode(p3.at[h, k], p3m.at[h, k])
        value = value / weight(h, spot.unit(0, 0))
        new = cell[pl.ds(h * prow, prow), :] * value / sums_of["total"]
        two.place(h, 0, 0)[...] = new.astype(BF)
        two.start(h)
        cell_new[pl.ds(h * prow, prow), :] = new
        sums_of[h] = jnp.sum(new, axis=0, keepdims=True)
        if all(i in sums_of for i in range(PARTS)):
            total = sums_of[0]
            for i in range(1, PARTS):
                total = total + sums_of[i]
            next_sum[...] = total
            next_parts[spot.me] = total
            sums_of["shared"] = share(next_sum, next_parts, ns, nr)

    def second(units, j):
        total = acc[j]
        for h, k, e in units:
            ratio, rows_bf = ratio_of(next_cell, h, spot.unit(k, e), j)
            total = total + lax.dot_general(
                ratio, rows_bf, (((0,), (0,)), ((), ())), preferred_element_type=F32
            )
        acc[j] = total

    order = Plan(far, near).build()
    seconds = [task[1:] for task in order if task[0] == "second"]
    late = seconds[-LAST:]
    for task in order:
        kind = task[0]
        if kind in ("one", "two"):
            side = one if kind == "one" else two
            if task[1] == "far":
                side.take_far(*task[2:])
            else:
                side.take_near(*task[2:])
        elif kind == "first":
            first(*task[1:])
        elif kind == "mix":
            mix(*task[1:])
        elif kind == "sum":
            stage_sum(*task[1:])
        elif kind == "fresh":
            fresh(*task[1:])
        elif task[1:] not in late:
            two.ready(*task[1:])
            for j in range(tiles):
                second([task[1:]], j)
    for task in late:
        two.ready(*task)

    def balance(j):
        return jnp.mean(gene_bf[j].astype(F32), axis=1, keepdims=True)

    mine = lax.axis_index("cell")
    sum_copies, copies = {}, {}
    for j in range(tiles):
        second(late, j)
        encode(acc[j] * balance(j), code.at[j], codem.at[j])
        for d in range(1, cells):
            where = {"cell": lax.rem(mine + d, cells)}
            copies[j, d] = (
                send(code.at[j], other.at[mine, j], fs.at[d, j], fr.at[d, j], where),
                send(codem.at[j], otherm.at[mine, j], uf.at[d, j], vf.at[d, j], where),
            )
        other[mine, j] = code[j]
        otherm[mine, j] = codem[j]
        if j == 0:
            for copy in sums_of["shared"]:
                copy.wait()
            sums = jnp.sum(next_parts[...], axis=0)
            group_sum[...] = sums
            other_sum[mine] = sums
            for d in range(1, cells):
                sum_copies[d] = send(group_sum, other_sum.at[mine], os.at[d], orr.at[d],
                                     {"cell": lax.rem(mine + d, cells)})
    for d in range(1, cells):
        sum_copies[d].wait()
    sums = other_sum[0]
    for k in range(1, cells):
        sums += other_sum[k]
    for j in range(tiles):
        for d in range(1, cells):
            for copy in copies[j, d]:
                copy.wait()
        value = decode(other.at[0, j], otherm.at[0, j])
        for k in range(1, cells):
            value += decode(other.at[k, j], otherm.at[k, j])
        gene_new[j] = gene[j] * (value / balance(j)) / sums
    for copy in [*one.copies(), *two.copies(), *c1.values()]:
        copy.wait_send()
    for pair in [*c2.values(), *c3.values()]:
        for copy in pair:
            copy.wait_send()


VMEM = pl.BlockSpec(memory_space=pltpu.VMEM)
SMEM = pl.BlockSpec(memory_space=pltpu.SMEM)
ANY = pl.BlockSpec(memory_space=pl.ANY)


def step(group, cells, blocks, brow, bcol, bcount, cell, gene):
    far, near, cores = digits(group)
    slots, width, _ = blocks.shape
    tiles, _, rank = gene.shape
    rows = cell.shape[0]
    prow = rows // PARTS
    spots = rows * group // width * tiles
    dma = pltpu.SemaphoreType.DMA
    vmem = pltpu.VMEM
    hke = (PARTS, far, near)
    return pl.pallas_call(
        functools.partial(step_kernel, group, cells),
        out_shape=(vmem(cell.shape, F32), vmem(gene.shape, F32)),
        in_specs=[ANY, VMEM, VMEM, SMEM, ANY, ANY],
        out_specs=(VMEM, VMEM),
        scratch_shapes=[
            vmem((slots + 1, width, width), BF),
            vmem((spots, 128), I32),
            pltpu.SMEM((spots, 128), I32),
            vmem((rows, rank), F32),
            vmem((tiles, width, rank), F32),
            vmem((tiles, width, rank), BF),
            vmem((tiles, rank, width), BF),
            vmem((1, rank), F32),
            vmem((group, 1, rank), F32),
            vmem((PARTS, far * near, cores * prow, rank), BF),
            vmem((1, rank), F32),
            vmem((group, 1, rank), F32),
            vmem((PARTS, far * near, cores * prow, rank), BF),
            vmem((PARTS, far * near, cores * prow, rank), F32),
            vmem((*hke, prow, rank), F32),
            vmem((*hke, prow, rank), I16),
            vmem((PARTS, far, prow, rank), I16),
            vmem((*hke, prow, rank), I16),
            vmem((PARTS, far, prow, rank), I16),
            vmem((*hke, 1, rank), F32),
            vmem((PARTS, far, 1, rank), F32),
            vmem((*hke, 1, rank), F32),
            vmem((PARTS, far, 1, rank), F32),
            vmem((tiles, width, rank), F32),
            vmem((tiles, width, rank), I16),
            vmem((tiles, 1, rank), F32),
            vmem((cells, tiles, width, rank), I16),
            vmem((cells, tiles, 1, rank), F32),
            vmem((1, rank), F32),
            vmem((cells, 1, rank), F32),
        ] + gather_sems(far, near) * 2 + [dma(hke)] * 4 + [dma((PARTS, far))] * 2
        + [dma((group,))] * 4 + [dma((cells, tiles))] * 2 + [dma((cells,))] * 2 + [dma((4,))]
        + [dma(hke)] * 2 + [dma((PARTS, far))] * 2 + [dma((cells, tiles))] * 2,
        compiler_params=pltpu.CompilerParams(
            collective_id=0, has_side_effects=True, vmem_limit_bytes=60 * 1024 * 1024
        ),
        name="update_step",
    )(blocks, brow, bcol, bcount, cell, gene)


def on_device(cells, group, blocks, brow, bcol, bcount, cell_factor, gene_factor):
    _, width, _ = blocks.shape
    rank = cell_factor.shape[-1]
    tiles = gene_factor.shape[0] // width
    cell_new, gene_new = step(group, cells, blocks, brow.reshape(1, -1), bcol.reshape(1, -1), bcount,
                              cell_factor, gene_factor.reshape(tiles, width, rank))
    return cell_new, gene_new.reshape(gene_factor.shape)


def solution(mesh):
    sizes = dict(mesh.shape)
    placed = (
        P(("cell", "gene"), None, None),
        P(("cell", "gene")),
        P(("cell", "gene")),
        P(("cell", "gene")),
        P(("cell", "gene"), None),
        P("gene", None),
    )
    return jax.shard_map(
        functools.partial(on_device, sizes["cell"], sizes["gene"]),
        mesh=mesh,
        in_specs=placed,
        out_specs=(P(("cell", "gene"), None), P("gene", None)),
        check_vma=False,
    )
```

```python
import functools

import jax
import jax.numpy as jnp
from jax import lax
from jax.experimental import pallas as pl
from jax.experimental.pallas import tpu as pltpu
from jax.sharding import PartitionSpec as P

MESH = pl.DeviceIdType.MESH
F32 = jnp.float32
BF = jnp.bfloat16
I16 = jnp.int16
I32 = jnp.int32
CORES = 2
FAR = 4
PARTS = 2
LAST = 2
AHEAD = (1, 2, 3)
SPREAD = (3, 2, 1, 0)
PATIENCE = 0.0
COST = {"first": (1.24, 1.64), "second": (1.28, 1.8)}
WAIT = {"c": 0.95, "x": 2.2, "near": 2.6, "mid": 1.5}


def digits(group):
    return FAR, group // (FAR * CORES), CORES


def flip(v, k, n):
    if k == 0:
        return v
    if k == n - 1:
        return n - 1 - v
    if k == n // 2:
        return lax.rem(v + n // 2, n)
    return v + 1 - 2 * lax.rem(v, 2)


class Spot:
    def __init__(self, group):
        self.group = group
        self.far, self.near, self.cores = digits(group)
        self.me = lax.axis_index("gene")
        self.a = self.me // (self.near * self.cores)
        self.b = lax.rem(self.me // self.cores, self.near)
        self.c = lax.rem(self.me, self.cores)

    def unit(self, k, e):
        return flip(self.a, k, self.far) * self.near + flip(self.b, e, self.near)

    def peer(self, k, e, core):
        return {"gene": self.unit(k, e) * self.cores + core}


def send(src, dst, send_sem, recv_sem, where):
    copy = pltpu.make_async_remote_copy(
        src_ref=src, dst_ref=dst, send_sem=send_sem, recv_sem=recv_sem,
        device_id=where, device_id_type=MESH,
    )
    copy.start()
    return copy


def drain(ref, sem):
    pltpu.make_async_copy(ref, ref, sem).wait()


def greet(axis, size):
    barrier = pltpu.get_barrier_semaphore()
    me = lax.axis_index(axis)
    for d in range(1, size):
        pl.semaphore_signal(
            barrier, inc=1, device_id={axis: lax.rem(me + d, size)}, device_id_type=MESH
        )


def encode(value, code, scale):
    top = jnp.max(jnp.abs(value), axis=0, keepdims=True)
    factor = jnp.where(top > 0.0, 32767.0 / top, 0.0)
    code[...] = jnp.round(value * factor).astype(jnp.int32).astype(jnp.int16)
    scale[...] = top * (1.0 / 32767.0)


def decode(code, scale):
    return code[...].astype(jnp.int32).astype(F32) * scale[...]


class Gather:
    def __init__(self, spot, out, prow, sems):
        self.spot, self.out, self.prow = spot, out, prow
        self.sent, self.zr, self.xr, self.cr = sems
        self.zc, self.xc, self.cc = {}, {}, {}

    def place(self, h, k, e):
        spot = self.spot
        first = pl.multiple_of(spot.c * self.prow, self.prow)
        return self.out.at[h, spot.unit(k, e), pl.ds(first, self.prow)]

    def start(self, h):
        spot, src = self.spot, self.place(h, 0, 0)
        for k in AHEAD:
            self.zc[h, k] = send(src, src, self.sent.at[0], self.zr.at[h, k - 1],
                                 spot.peer(k, 0, spot.c))
        self.forward(h, 0)

    def forward(self, h, k):
        spot, src = self.spot, self.place(h, k, 0)
        for e in range(1, spot.near):
            self.xc[h, k, e] = send(src, src, self.sent.at[1], self.xr.at[h, k, e - 1],
                                    spot.peer(0, e, spot.c))
        self.pair(h, k, 0)

    def pair(self, h, k, e):
        spot, src = self.spot, self.place(h, k, e)
        self.cc[h, k, e] = send(src, src, self.sent.at[2], self.cr.at[h, k, e],
                                spot.peer(0, 0, 1 - spot.c))

    def take_far(self, h, k):
        self.zc[h, k].wait_recv()
        self.forward(h, k)

    def take_near(self, h, k, e):
        self.xc[h, k, e].wait_recv()
        self.pair(h, k, e)

    def ready(self, h, k, e):
        self.cc[h, k, e].wait_recv()

    def close(self):
        far, near = self.spot.far, self.spot.near
        for i, units in enumerate((far - 1, far * (near - 1), far * near)):
            drain(self.out.at[0, pl.ds(0, units)], self.sent.at[i])


def gather_sems(far, near):
    dma = pltpu.SemaphoreType.DMA
    return [dma((3,)), dma((PARTS, far - 1)), dma((PARTS, far, near - 1)), dma((PARTS, far, near))]


class Plan:
    def __init__(self, far, near):
        self.far, self.near = far, near
        self.time = 0.0
        self.free = {"c": 0.0, "x": 0.0, "near": 0.0, "mid": 0.0}
        self.arrive = {}
        self.order = []

    def post(self, key, k, e):
        link = "x" if e else ("c", "near", "mid", "mid")[k]
        wire = {"c": 0.1, "x": 1.4, "near": 1.4, "mid": 2.8}[link] / PARTS
        self.free[link] = max(self.time, self.free[link]) + wire
        self.arrive[key] = self.free[link] + WAIT[link]

    def begin(self, name, h):
        for k in AHEAD:
            self.post((name, "z", h, k), k, 0)
        self.ahead(name, h, 0)

    def ahead(self, name, h, k):
        for e in range(1, self.near):
            self.post((name, "x", h, k, e), 0, e)
        self.post((name, "c", h, k, 0), 0, 0)

    def tasks(self):
        far, near, parts = range(self.far), range(self.near), range(PARTS)
        mixed = [("p2", h, k, e) for h in parts for k in far for e in near[1:]]
        out = []
        for h in parts:
            out += [((name, "far", h, k), [(name, "z", h, k)], 0.02)
                    for name in ("one", "two") for k in far[1:]]
        for h in parts:
            need = [("p1", h, 0, 0)] + [("p3", h, k) for k in far[1:]]
            need += [key for key in mixed if key[1] == h and key[2] == 0]
            out.append((("fresh", h), need, 0.35))
        for h in parts:
            for k in reversed(far[1:]):
                need = [("p1", h, k, 0)]
                need += [key for key in mixed if key[1:3] == (h, k)]
                out.append((("sum", h, k), need, 0.15))
        for h in parts:
            out += [(("mix", h, k, e), [("p1", h, k, e)], 0.14)
                    for k in reversed(far) for e in near[1:]]
        for h in parts:
            out += [((name, "near", h, k, e), [(name, "x", h, k, e)], 0.02)
                    for name in ("one", "two") for k in far for e in near[1:]]
        spread = [(h, k, e) for h in parts for e in reversed(near) for k in SPREAD]
        for name, side in (("first", "one"), ("second", "two")):
            out += [((name, u), [(side, "c", *u)], COST[name][0] / PARTS) for u in spread]
        return out

    def run(self, task):
        kind = task[0]
        if kind == "first":
            for unit in task[1:]:
                self.post(("p1", *unit), 0, 0)
        elif kind == "mix":
            h, k, e = task[1:]
            self.post(("p2", h, k, e), 0, e)
        elif kind == "sum":
            self.post(("p3", *task[1:]), task[2], 0)
        elif kind == "fresh":
            self.begin("two", task[1])
        elif kind in ("one", "two") and task[1] == "far":
            self.ahead(kind, task[2], task[3])
        elif kind in ("one", "two"):
            self.post((kind, "c", *task[2:]), 0, 0)

    def build(self):
        for h in range(PARTS):
            self.begin("one", h)
        self.time = 0.5
        left = self.tasks()
        while left:
            known = [(max(self.arrive[n] for n in need), i) for i, (_, need, _) in enumerate(left)
                     if all(n in self.arrive for n in need)]
            ready = [i for when, i in known if when <= self.time]
            if not ready:
                self.time = min(when for when, _ in known)
                continue
            pick = min(ready)
            kind = left[pick][0][0]
            if kind in COST:
                alike = sorted((max(when, self.time), i) for when, i in known
                               if left[i][0][0] == kind and i != pick)
                soon = [when for when, _ in known if when > self.time]
                if alike and alike[0][0] > self.time and min(soon) <= self.time + PATIENCE:
                    self.time = min(soon)
                    continue
                if alike and alike[0][0] <= self.time:
                    other = alike[0][1]
                    units = left[pick][0][1:] + left[other][0][1:]
                    for i in sorted((pick, other), reverse=True):
                        left.pop(i)
                    left.insert(0, ((kind, *units), [], COST[kind][1] / PARTS))
                    pick = 0
            task, _, cost = left.pop(pick)
            self.time += cost
            self.run(task)
            self.order.append(task)
        return self.order


def step_kernel(group, cells, blocks, brow_in, bcol_in, bcount_in, cell_in, gene_in, cell_new,
                gene_new, brow, bcol, bcount, held, spread, table, cell, gene, gene_bf, flipped, own_sum, parts, cell_bf,
                next_sum, next_parts, next_cell, numer, p1, p2, p3, t2, t3,
                p2m, p3m, t2m, t3m, acc, code, codem, other, otherm, group_sum, other_sum, *sems):
    spot = Spot(group)
    far, near, cores = spot.far, spot.near, spot.cores
    c = spot.c
    slots, width, _ = blocks.shape
    tiles = gene.shape[0]
    rows = cell.shape[0]
    prow = rows // PARTS
    sub = width // rows
    one_sems, two_sems = sems[0:4], sems[4:8]
    sent, r1, r2, v2, r3, v3, gr, nr, fr, vf, orr, ls = sems[8:]
    s1, s2, u2, s3, u3, gs, ns, fs, uf, os = (sent.at[i] for i in range(10))
    greet("gene", group)
    greet("cell", cells)
    load_cell = pltpu.make_async_copy(cell_in, cell, ls.at[0])
    load_cell.start()
    small = [pltpu.make_async_copy(src, dst, ls.at[4 + i])
             for i, (src, dst) in enumerate(((brow_in, brow), (bcol_in, bcol), (bcount_in, bcount)))]
    for copy in small:
        copy.start()
    load_gene = pltpu.make_async_copy(gene_in, gene, ls.at[1])
    load_gene.start()
    load = pltpu.make_async_copy(blocks, held.at[pl.ds(0, slots)], ls.at[2])
    load.start()

    held[slots] = jnp.zeros((width, width), BF)
    for copy in small:
        copy.wait()
    lane = lax.broadcasted_iota(I32, (1, slots), 1)
    where = jnp.where(lane < bcount[0], brow[...] * tiles + bcol[...], -1)
    at = lax.broadcasted_iota(I32, (spread.shape[0], slots), 0)
    found = jnp.min(jnp.where(at == where, lane, slots), axis=1, keepdims=True)
    spread[...] = jnp.broadcast_to(found, spread.shape)
    load_table = pltpu.make_async_copy(spread, table, ls.at[3])
    load_table.start()

    one = Gather(spot, cell_bf, prow, one_sems)
    two = Gather(spot, next_cell, prow, two_sems)
    load_cell.wait()
    for h in range(PARTS):
        one.place(h, 0, 0)[...] = cell[pl.ds(h * prow, prow), :].astype(BF)
    pl.semaphore_wait(pltpu.get_barrier_semaphore(), group - 1 + cells - 1)
    for h in range(PARTS):
        one.start(h)

    def share(src, out, ss, sr):
        for d in range(1, group):
            send(src, out.at[spot.me], ss, sr.at[0], {"gene": lax.rem(spot.me + d, group)})

    load_gene.wait()
    first_sum = jnp.zeros((1, gene.shape[-1]), F32)
    for j in range(tiles):
        first_sum += jnp.sum(gene[j], axis=0, keepdims=True)
    own_sum[...] = first_sum
    parts[spot.me] = first_sum
    share(own_sum, parts, gs, gr)
    for j in range(tiles):
        gene_bf[j] = gene[j].astype(BF)
        flipped[j] = gene[j].astype(BF).T
    acc[...] = jnp.zeros_like(acc)
    load_table.wait()
    load.wait()

    def rows_of(source, units):
        return jnp.concatenate([source[h, spot.unit(k, e)] for h, k, e in units], axis=0)

    def ratio_of(rows_bf, units, j):
        found = []
        for h, k, e in units:
            for core in range(cores):
                g = spot.unit(k, e) * cores + core
                slot = table[(g // sub) * tiles + j, 0]
                if sub == 1:
                    found.append(held[slot, pl.ds(h * prow, prow), :])
                else:
                    first = pl.multiple_of(lax.rem(g, sub) * rows + h * prow, prow)
                    found.append(held[slot, pl.ds(first, prow), :])
        x = jnp.concatenate(found, axis=0)
        model = jnp.dot(rows_bf, flipped[j], preferred_element_type=F32)
        return (x.astype(F32) / model).astype(BF)

    c1, c2, c3 = {}, {}, {}
    mine_at = pl.ds(pl.multiple_of(c * prow, prow), prow)
    theirs_at = pl.ds(pl.multiple_of((1 - c) * prow, prow), prow)

    def first(*units):
        for unit in units:
            one.ready(*unit)
        rows_bf = rows_of(cell_bf, units)
        total = None
        for j in range(tiles):
            ratio = ratio_of(rows_bf, units, j)
            term = jnp.dot(ratio, gene_bf[j], preferred_element_type=F32)
            total = term if total is None else total + term
        for i, (h, k, e) in enumerate(units):
            u = spot.unit(k, e)
            numer[h, u] = total[i * cores * prow:(i + 1) * cores * prow]
            c1[h, k, e] = send(numer.at[h, u, theirs_at], p1.at[h, k, e], s1,
                               r1.at[h, k, e], spot.peer(0, 0, 1 - c))

    def weight(h, u):
        return jnp.mean(cell_bf[h, u, mine_at].astype(F32), axis=1, keepdims=True)

    def both(h, k, e):
        c1[h, k, e].wait_recv()
        u = spot.unit(k, e)
        return (numer[h, u, mine_at] + p1[h, k, e]) * weight(h, u)

    def mix(h, k, e):
        encode(both(h, k, e), t2.at[h, k, e], t2m.at[h, k, e])
        where = spot.peer(0, e, c)
        c2[h, k, e] = (
            send(t2.at[h, k, e], p2.at[h, k, e], s2, r2.at[h, k, e - 1], where),
            send(t2m.at[h, k, e], p2m.at[h, k, e], u2, v2.at[h, k, e - 1], where),
        )

    def summed(h, k):
        value = both(h, k, 0)
        for e in range(1, near):
            for copy in c2[h, k, e]:
                copy.wait_recv()
            value += decode(p2.at[h, k, e], p2m.at[h, k, e])
        return value

    def stage_sum(h, k):
        encode(summed(h, k), t3.at[h, k], t3m.at[h, k])
        where = spot.peer(k, 0, c)
        c3[h, k] = (
            send(t3.at[h, k], p3.at[h, k], s3, r3.at[h, k - 1], where),
            send(t3m.at[h, k], p3m.at[h, k], u3, v3.at[h, k - 1], where),
        )

    sums_of = {}

    def fresh(h):
        if "total" not in sums_of:
            drain(parts.at[pl.ds(0, group - 1)], gr.at[0])
            sums_of["total"] = jnp.sum(parts[...], axis=0)
        value = summed(h, 0)
        for k in range(1, far):
            for copy in c3[h, k]:
                copy.wait_recv()
            value += decode(p3.at[h, k], p3m.at[h, k])
        value = value / weight(h, spot.unit(0, 0))
        new = cell[pl.ds(h * prow, prow), :] * value / sums_of["total"]
        two.place(h, 0, 0)[...] = new.astype(BF)
        two.start(h)
        cell_new[pl.ds(h * prow, prow), :] = new
        sums_of[h] = jnp.sum(new, axis=0, keepdims=True)
        if all(i in sums_of for i in range(PARTS)):
            total = sums_of[0]
            for i in range(1, PARTS):
                total = total + sums_of[i]
            next_sum[...] = total
            next_parts[spot.me] = total
            share(next_sum, next_parts, ns, nr)

    def second(units, rows_bf, j):
        ratio = ratio_of(rows_bf, units, j)
        acc[j] += lax.dot_general(
            ratio, rows_bf, (((0,), (0,)), ((), ())), preferred_element_type=F32
        )

    order = Plan(far, near).build()
    late = [unit for task in order if task[0] == "second" for unit in task[1:]][-LAST:]
    for task in order:
        kind = task[0]
        if kind in ("one", "two"):
            side = one if kind == "one" else two
            if task[1] == "far":
                side.take_far(*task[2:])
            else:
                side.take_near(*task[2:])
        elif kind == "first":
            first(*task[1:])
        elif kind == "mix":
            mix(*task[1:])
        elif kind == "sum":
            stage_sum(*task[1:])
        elif kind == "fresh":
            fresh(*task[1:])
        else:
            units = [unit for unit in task[1:] if unit not in late]
            for unit in units:
                two.ready(*unit)
            rows_bf = rows_of(next_cell, units) if units else None
            for j in range(tiles if units else 0):
                second(units, rows_bf, j)
    for unit in late:
        two.ready(*unit)
    late_rows = rows_of(next_cell, late)

    def balance(j):
        return jnp.mean(gene_bf[j].astype(F32), axis=1, keepdims=True)

    mine = lax.axis_index("cell")
    sum_copies, copies = {}, {}
    for j in range(tiles):
        second(late, late_rows, j)
        encode(acc[j] * balance(j), code.at[j], codem.at[j])
        for d in range(1, cells):
            where = {"cell": lax.rem(mine + d, cells)}
            copies[j, d] = (
                send(code.at[j], other.at[mine, j], fs, fr.at[d - 1, j], where),
                send(codem.at[j], otherm.at[mine, j], uf, vf.at[d - 1, j], where),
            )
        other[mine, j] = code[j]
        otherm[mine, j] = codem[j]
        if j == 0:
            drain(next_parts.at[pl.ds(0, group - 1)], nr.at[0])
            sums = jnp.sum(next_parts[...], axis=0)
            group_sum[...] = sums
            other_sum[mine] = sums
            for d in range(1, cells):
                sum_copies[d] = send(group_sum, other_sum.at[mine], os, orr.at[d - 1],
                                     {"cell": lax.rem(mine + d, cells)})
    for d in range(1, cells):
        sum_copies[d].wait_recv()
    sums = other_sum[0]
    for k in range(1, cells):
        sums += other_sum[k]
    for j in range(tiles):
        for d in range(1, cells):
            for copy in copies[j, d]:
                copy.wait_recv()
        value = decode(other.at[0, j], otherm.at[0, j])
        for k in range(1, cells):
            value += decode(other.at[k, j], otherm.at[k, j])
        gene_new[j] = gene[j] * (value / balance(j)) / sums
    one.close()
    two.close()
    drain(numer.at[0], s1)
    drain(t2.at[:, :, 0:near - 1], s2)
    drain(t2m.at[:, :, 0:near - 1], u2)
    drain(t3.at[:, 1:far], s3)
    drain(t3m.at[:, 1:far], u3)
    drain(parts.at[pl.ds(0, group - 1)], gs)
    drain(next_parts.at[pl.ds(0, group - 1)], ns)
    drain(other.at[0:cells - 1], fs)
    drain(otherm.at[0:cells - 1], uf)
    drain(other_sum.at[0:cells - 1], os)


VMEM = pl.BlockSpec(memory_space=pltpu.VMEM)
HBM = pl.BlockSpec(memory_space=pltpu.HBM)


def step(group, cells, blocks, brow, bcol, bcount, cell, gene):
    far, near, cores = digits(group)
    slots, width, _ = blocks.shape
    tiles, _, rank = gene.shape
    rows = cell.shape[0]
    prow = rows // PARTS
    spots = rows * group // width * tiles
    dma = pltpu.SemaphoreType.DMA
    vmem = pltpu.VMEM
    hke = (PARTS, far, near)
    return pl.pallas_call(
        functools.partial(step_kernel, group, cells),
        out_shape=(vmem(cell.shape, F32), vmem(gene.shape, F32)),
        in_specs=[HBM] * 6,
        out_specs=(VMEM, VMEM),
        scratch_shapes=[
            vmem((1, slots), I32),
            vmem((1, slots), I32),
            pltpu.SMEM((1,), I32),
            vmem((slots + 1, width, width), BF),
            vmem((spots, 128), I32),
            pltpu.SMEM((spots, 128), I32),
            vmem((rows, rank), F32),
            vmem((tiles, width, rank), F32),
            vmem((tiles, width, rank), BF),
            vmem((tiles, rank, width), BF),
            vmem((1, rank), F32),
            vmem((group, 1, rank), F32),
            vmem((PARTS, far * near, cores * prow, rank), BF),
            vmem((1, rank), F32),
            vmem((group, 1, rank), F32),
            vmem((PARTS, far * near, cores * prow, rank), BF),
            vmem((PARTS, far * near, cores * prow, rank), F32),
            vmem((*hke, prow, rank), F32),
            vmem((*hke, prow, rank), I16),
            vmem((PARTS, far, prow, rank), I16),
            vmem((*hke, prow, rank), I16),
            vmem((PARTS, far, prow, rank), I16),
            vmem((*hke, 1, rank), F32),
            vmem((PARTS, far, 1, rank), F32),
            vmem((*hke, 1, rank), F32),
            vmem((PARTS, far, 1, rank), F32),
            vmem((tiles, width, rank), F32),
            vmem((tiles, width, rank), I16),
            vmem((tiles, 1, rank), F32),
            vmem((cells, tiles, width, rank), I16),
            vmem((cells, tiles, 1, rank), F32),
            vmem((1, rank), F32),
            vmem((cells, 1, rank), F32),
        ] + gather_sems(far, near) * 2 + [dma((10,)), dma(hke)]
        + [dma((PARTS, far, near - 1))] * 2 + [dma((PARTS, far - 1))] * 2 + [dma((1,))] * 2
        + [dma((cells - 1, tiles))] * 2 + [dma((cells - 1,)), dma((7,))],
        compiler_params=pltpu.CompilerParams(
            collective_id=0, has_side_effects=True, vmem_limit_bytes=60 * 1024 * 1024
        ),
        name="update_step",
    )(blocks, brow, bcol, bcount, cell, gene)


def on_device(cells, group, blocks, brow, bcol, bcount, cell_factor, gene_factor):
    _, width, _ = blocks.shape
    rank = cell_factor.shape[-1]
    tiles = gene_factor.shape[0] // width
    cell_new, gene_new = step(group, cells, blocks, brow.reshape(1, -1), bcol.reshape(1, -1), bcount,
                              cell_factor, gene_factor.reshape(tiles, width, rank))
    return cell_new, gene_new.reshape(gene_factor.shape)


def solution(mesh):
    sizes = dict(mesh.shape)
    placed = (
        P(("cell", "gene"), None, None),
        P(("cell", "gene")),
        P(("cell", "gene")),
        P(("cell", "gene")),
        P(("cell", "gene"), None),
        P("gene", None),
    )
    return jax.shard_map(
        functools.partial(on_device, sizes["cell"], sizes["gene"]),
        mesh=mesh,
        in_specs=placed,
        out_specs=(P(("cell", "gene"), None), P("gene", None)),
        check_vma=False,
    )
```

```python
import functools

import jax
import jax.numpy as jnp
from jax import lax
from jax.experimental import pallas as pl
from jax.experimental.pallas import tpu as pltpu
from jax.sharding import PartitionSpec as P

MESH = pl.DeviceIdType.MESH
F32 = jnp.float32
BF = jnp.bfloat16
I16 = jnp.int16
I32 = jnp.int32
CORES = 2
FAR = 4
PARTS = 2
LAST = 2
AHEAD = (1, 2, 3)
DIRECT = {"one": (), "sum": (), "two": ((0, 1), (1, 1))}
SPREAD = (3, 2, 1, 0)
PATIENCE = 0.0
COST = {"first": (1.24, 1.64), "second": (1.28, 1.8)}
WAIT = {"c": 0.95, "x": 2.2, "near": 2.6, "mid": 1.5}


def digits(group):
    return FAR, group // (FAR * CORES), CORES


def flip(v, k, n):
    if k == 0:
        return v
    if k == n - 1:
        return n - 1 - v
    if k == n // 2:
        return lax.rem(v + n // 2, n)
    return v + 1 - 2 * lax.rem(v, 2)


class Spot:
    def __init__(self, group):
        self.group = group
        self.far, self.near, self.cores = digits(group)
        self.me = lax.axis_index("gene")
        self.a = self.me // (self.near * self.cores)
        self.b = lax.rem(self.me // self.cores, self.near)
        self.c = lax.rem(self.me, self.cores)

    def unit(self, k, e):
        return flip(self.a, k, self.far) * self.near + flip(self.b, e, self.near)

    def peer(self, k, e, core):
        return {"gene": self.unit(k, e) * self.cores + core}


def send(src, dst, send_sem, recv_sem, where):
    copy = pltpu.make_async_remote_copy(
        src_ref=src, dst_ref=dst, send_sem=send_sem, recv_sem=recv_sem,
        device_id=where, device_id_type=MESH,
    )
    copy.start()
    return copy


def drain(ref, sem):
    pltpu.make_async_copy(ref, ref, sem).wait()


def greet(axis, size):
    barrier = pltpu.get_barrier_semaphore()
    me = lax.axis_index(axis)
    for d in range(1, size):
        pl.semaphore_signal(
            barrier, inc=1, device_id={axis: lax.rem(me + d, size)}, device_id_type=MESH
        )


def encode(value, code, scale):
    top = jnp.max(jnp.abs(value), axis=0, keepdims=True)
    factor = jnp.where(top > 0.0, 32767.0 / top, 0.0)
    code[...] = jnp.round(value * factor).astype(jnp.int32).astype(jnp.int16)
    scale[...] = top * (1.0 / 32767.0)


def decode(code, scale):
    return code[...].astype(jnp.int32).astype(F32) * scale[...]


class Gather:
    def __init__(self, spot, out, prow, direct, sems):
        self.direct = direct
        self.spot, self.out, self.prow = spot, out, prow
        self.sent, self.zr, self.xr, self.cr = sems
        self.zc, self.xc, self.cc = {}, {}, {}

    def place(self, h, k, e):
        spot = self.spot
        first = pl.multiple_of(spot.c * self.prow, self.prow)
        return self.out.at[h, spot.unit(k, e), pl.ds(first, self.prow)]

    def start(self, h):
        spot, src = self.spot, self.place(h, 0, 0)
        for k in AHEAD:
            self.zc[h, k] = send(src, src, self.sent.at[0], self.zr.at[h, k - 1],
                                 spot.peer(k, 0, spot.c))
        self.forward(h, 0)
        for k in AHEAD:
            for e in range(1, spot.near if (h, k) in self.direct else 1):
                self.xc[h, k, e] = send(src, src, self.sent.at[1], self.xr.at[h, k, e - 1],
                                        spot.peer(k, e, spot.c))

    def forward(self, h, k):
        spot, src = self.spot, self.place(h, k, 0)
        for e in range(1, 1 if (h, k) in self.direct else spot.near):
            self.xc[h, k, e] = send(src, src, self.sent.at[1], self.xr.at[h, k, e - 1],
                                    spot.peer(0, e, spot.c))
        self.pair(h, k, 0)

    def pair(self, h, k, e):
        spot, src = self.spot, self.place(h, k, e)
        self.cc[h, k, e] = send(src, src, self.sent.at[2], self.cr.at[h, k, e],
                                spot.peer(0, 0, 1 - spot.c))

    def take_far(self, h, k):
        self.zc[h, k].wait_recv()
        self.forward(h, k)

    def take_near(self, h, k, e):
        self.xc[h, k, e].wait_recv()
        self.pair(h, k, e)

    def ready(self, h, k, e):
        self.cc[h, k, e].wait_recv()

    def close(self):
        far, near = self.spot.far, self.spot.near
        for i, units in enumerate((far - 1, far * (near - 1), far * near)):
            drain(self.out.at[0, pl.ds(0, units)], self.sent.at[i])


def gather_sems(far, near):
    dma = pltpu.SemaphoreType.DMA
    return [dma((3,)), dma((PARTS, far - 1)), dma((PARTS, far, near - 1)), dma((PARTS, far, near))]


class Plan:
    def __init__(self, far, near):
        self.far, self.near = far, near
        self.time = 0.0
        self.free = {"c": 0.0, "x": 0.0, "near": 0.0, "mid": 0.0}
        self.arrive = {}
        self.order = []

    def post(self, key, k, e):
        link = ("x" if e else "c", "near", "mid", "mid")[k]
        wire = {"c": 0.1, "x": 1.4, "near": 1.4, "mid": 2.8}[link] / PARTS
        self.free[link] = max(self.time, self.free[link]) + wire
        self.arrive[key] = self.free[link] + WAIT[link] + (0.7 if k and e else 0.0)

    def begin(self, name, h):
        for k in AHEAD:
            self.post((name, "z", h, k), k, 0)
        self.ahead(name, h, 0)
        for k in AHEAD:
            for e in range(1, self.near if (h, k) in DIRECT[name] else 1):
                self.post((name, "x", h, k, e), k, e)

    def ahead(self, name, h, k):
        for e in range(1, 1 if (h, k) in DIRECT[name] else self.near):
            self.post((name, "x", h, k, e), 0, e)
        self.post((name, "c", h, k, 0), 0, 0)

    def tasks(self):
        far, near, parts = range(self.far), range(self.near), range(PARTS)
        mixed = [("p2", h, k, e) for h in parts for k in far for e in near[1:]]
        out = []
        for h in parts:
            out += [((name, "far", h, k), [(name, "z", h, k)], 0.02)
                    for name in ("one", "two") for k in far[1:]]
        for h in parts:
            need = [("p1", h, 0, 0)] + [("p3", h, k) for k in far[1:]]
            need += [key for key in mixed if key[1] == h and (key[2] == 0 or (h, key[2]) in DIRECT["sum"])]
            out.append((("fresh", h), need, 0.35))
        for h in parts:
            for k in reversed(far[1:]):
                need = [("p1", h, k, 0)]
                need += [key for key in mixed if key[1:3] == (h, k) and (h, k) not in DIRECT["sum"]]
                out.append((("sum", h, k), need, 0.15))
        for h in parts:
            out += [(("mix", h, k, e), [("p1", h, k, e)], 0.14)
                    for k in reversed(far) for e in near[1:]]
        for h in parts:
            out += [((name, "near", h, k, e), [(name, "x", h, k, e)], 0.02)
                    for name in ("one", "two") for k in far for e in near[1:]]
        spread = [(h, k, e) for h in parts for e in reversed(near) for k in SPREAD]
        for name, side in (("first", "one"), ("second", "two")):
            out += [((name, u), [(side, "c", *u)], COST[name][0] / PARTS) for u in spread]
        return out

    def run(self, task):
        kind = task[0]
        if kind == "first":
            for unit in task[1:]:
                self.post(("p1", *unit), 0, 0)
        elif kind == "mix":
            h, k, e = task[1:]
            self.post(("p2", h, k, e), k if (h, k) in DIRECT["sum"] else 0, e)
        elif kind == "sum":
            self.post(("p3", *task[1:]), task[2], 0)
        elif kind == "fresh":
            self.begin("two", task[1])
        elif kind in ("one", "two") and task[1] == "far":
            self.ahead(kind, task[2], task[3])
        elif kind in ("one", "two"):
            self.post((kind, "c", *task[2:]), 0, 0)

    def build(self):
        for h in range(PARTS):
            self.begin("one", h)
        self.time = 0.5
        left = self.tasks()
        while left:
            known = [(max(self.arrive[n] for n in need), i) for i, (_, need, _) in enumerate(left)
                     if all(n in self.arrive for n in need)]
            ready = [i for when, i in known if when <= self.time]
            if not ready:
                self.time = min(when for when, _ in known)
                continue
            pick = min(ready)
            kind = left[pick][0][0]
            if kind in COST:
                alike = sorted((max(when, self.time), i) for when, i in known
                               if left[i][0][0] == kind and i != pick)
                soon = [when for when, _ in known if when > self.time]
                if alike and alike[0][0] > self.time and min(soon) <= self.time + PATIENCE:
                    self.time = min(soon)
                    continue
                if alike and alike[0][0] <= self.time:
                    other = alike[0][1]
                    units = left[pick][0][1:] + left[other][0][1:]
                    for i in sorted((pick, other), reverse=True):
                        left.pop(i)
                    left.insert(0, ((kind, *units), [], COST[kind][1] / PARTS))
                    pick = 0
            task, _, cost = left.pop(pick)
            self.time += cost
            self.run(task)
            self.order.append(task)
        return self.order


def step_kernel(group, cells, blocks, brow_in, bcol_in, bcount_in, cell_in, gene_in, cell_new,
                gene_new, brow, bcol, bcount, held, spread, table, cell, gene, gene_bf, flipped, own_sum, parts, cell_bf,
                next_sum, next_parts, next_cell, numer, p1, p2, p3, t2, t3,
                p2m, p3m, t2m, t3m, acc, code, codem, other, otherm, group_sum, other_sum, size, *sems):
    spot = Spot(group)
    far, near, cores = spot.far, spot.near, spot.cores
    c = spot.c
    slots, width, _ = blocks.shape
    tiles = gene.shape[0]
    rows = cell.shape[0]
    prow = rows // PARTS
    sub = width // rows
    one_sems, two_sems = sems[0:4], [sems[4], *sems[1:4]]
    sent, r1, r2, r3, gr, nr, fr, orr, ls = sems[5:]
    s1, s2, u2, s3, u3, gs, ns, fs, uf, os = (sent.at[i] for i in range(10))
    greet("gene", group)
    greet("cell", cells)
    load_cell = pltpu.make_async_copy(cell_in, cell, ls.at[0])
    load_cell.start()
    small = [pltpu.make_async_copy(src, dst, ls.at[4 + i])
             for i, (src, dst) in enumerate(((brow_in, brow), (bcol_in, bcol), (bcount_in, bcount)))]
    for copy in small:
        copy.start()
    load_gene = pltpu.make_async_copy(gene_in, gene, ls.at[1])
    load_gene.start()
    load = pltpu.make_async_copy(blocks, held.at[pl.ds(0, slots)], ls.at[2])
    load.start()

    held[slots] = jnp.zeros((width, width), BF)
    for copy in small:
        copy.wait()
    lane = lax.broadcasted_iota(I32, (1, slots), 1)
    where = jnp.where(lane < bcount[0], brow[...] * tiles + bcol[...], -1)
    at = lax.broadcasted_iota(I32, (spread.shape[0], slots), 0)
    found = jnp.min(jnp.where(at == where, lane, slots), axis=1, keepdims=True)
    spread[...] = jnp.broadcast_to(found, spread.shape)
    load_table = pltpu.make_async_copy(spread, table, ls.at[3])
    load_table.start()

    one = Gather(spot, cell_bf, prow, DIRECT["one"], one_sems)
    two = Gather(spot, next_cell, prow, DIRECT["two"], two_sems)
    load_cell.wait()
    for h in range(PARTS):
        one.place(h, 0, 0)[...] = cell[pl.ds(h * prow, prow), :].astype(BF)
    pl.semaphore_wait(pltpu.get_barrier_semaphore(), group - 1 + cells - 1)
    for h in range(PARTS):
        one.start(h)

    def share(src, out, ss, sr):
        for d in range(1, group):
            send(src, out.at[spot.me], ss, sr.at[0], {"gene": lax.rem(spot.me + d, group)})

    load_gene.wait()
    first_sum = jnp.zeros((1, gene.shape[-1]), F32)
    for j in range(tiles):
        first_sum += jnp.sum(gene[j], axis=0, keepdims=True)
    own_sum[...] = first_sum
    parts[spot.me] = first_sum
    share(own_sum, parts, gs, gr)
    for j in range(tiles):
        gene_bf[j] = gene[j].astype(BF)
        flipped[j] = gene[j].astype(BF).T
    acc[...] = jnp.zeros_like(acc)
    load_table.wait()
    load.wait()

    def rows_of(source, units):
        return jnp.concatenate([source[h, spot.unit(k, e)] for h, k, e in units], axis=0)

    def ratio_of(rows_bf, units, j):
        found = []
        for h, k, e in units:
            for core in range(cores):
                g = spot.unit(k, e) * cores + core
                slot = table[(g // sub) * tiles + j, 0]
                if sub == 1:
                    found.append(held[slot, pl.ds(h * prow, prow), :])
                else:
                    first = pl.multiple_of(lax.rem(g, sub) * rows + h * prow, prow)
                    found.append(held[slot, pl.ds(first, prow), :])
        x = jnp.concatenate(found, axis=0)
        model = jnp.dot(rows_bf, flipped[j], preferred_element_type=F32)
        return (x.astype(F32) / model).astype(BF)

    c1 = {}
    mine_at = pl.ds(pl.multiple_of(c * prow, prow), prow)
    theirs_at = pl.ds(pl.multiple_of((1 - c) * prow, prow), prow)

    def first(*units):
        for unit in units:
            one.ready(*unit)
        rows_bf = rows_of(cell_bf, units)
        total = None
        for j in range(tiles):
            ratio = ratio_of(rows_bf, units, j)
            term = jnp.dot(ratio, gene_bf[j], preferred_element_type=F32)
            total = term if total is None else total + term
        for i, (h, k, e) in enumerate(units):
            u = spot.unit(k, e)
            numer[h, u] = total[i * cores * prow:(i + 1) * cores * prow]
            c1[h, k, e] = send(numer.at[h, u, theirs_at], p1.at[h, k, e], s1,
                               r1.at[h, k, e], spot.peer(0, 0, 1 - c))

    def weight(h, u):
        return jnp.mean(cell_bf[h, u, mine_at].astype(F32), axis=1, keepdims=True)

    def both(h, k, e):
        c1[h, k, e].wait_recv()
        u = spot.unit(k, e)
        return (numer[h, u, mine_at] + p1[h, k, e]) * weight(h, u)

    def mix(h, k, e):
        encode(both(h, k, e), t2.at[h, k, e], t2m.at[h, k, e])
        where = spot.peer(k if (h, k) in DIRECT["sum"] else 0, e, c)
        send(t2.at[h, k, e], p2.at[h, k, e], s2, r2.at[h, k, e - 1], where)
        send(t2m.at[h, k, e], p2m.at[h, k, e], u2, r2.at[h, k, e - 1], where)

    def summed(h, k, mixed):
        value = both(h, k, 0)
        for i in mixed:
            for e in range(1, near):
                drain(size.at[pl.ds(0, prow // 2 + 1)], r2.at[h, i, e - 1])
                value += decode(p2.at[h, i, e], p2m.at[h, i, e])
        return value

    def stage_sum(h, k):
        encode(summed(h, k, () if (h, k) in DIRECT["sum"] else (k,)), t3.at[h, k], t3m.at[h, k])
        where = spot.peer(k, 0, c)
        send(t3.at[h, k], p3.at[h, k], s3, r3.at[h, k - 1], where)
        send(t3m.at[h, k], p3m.at[h, k], u3, r3.at[h, k - 1], where)

    sums_of = {}

    def fresh(h):
        if "total" not in sums_of:
            drain(parts.at[pl.ds(0, group - 1)], gr.at[0])
            sums_of["total"] = jnp.sum(parts[...], axis=0)
        value = summed(h, 0, [k for k in range(far) if k == 0 or (h, k) in DIRECT["sum"]])
        for k in range(1, far):
            drain(size.at[pl.ds(0, prow // 2 + 1)], r3.at[h, k - 1])
            value += decode(p3.at[h, k], p3m.at[h, k])
        value = value / weight(h, spot.unit(0, 0))
        new = cell[pl.ds(h * prow, prow), :] * value / sums_of["total"]
        two.place(h, 0, 0)[...] = new.astype(BF)
        two.start(h)
        cell_new[pl.ds(h * prow, prow), :] = new
        sums_of[h] = jnp.sum(new, axis=0, keepdims=True)
        if all(i in sums_of for i in range(PARTS)):
            total = sums_of[0]
            for i in range(1, PARTS):
                total = total + sums_of[i]
            next_sum[...] = total
            next_parts[spot.me] = total
            share(next_sum, next_parts, ns, nr)

    def second(units, rows_bf, j):
        ratio = ratio_of(rows_bf, units, j)
        acc[j] += lax.dot_general(
            ratio, rows_bf, (((0,), (0,)), ((), ())), preferred_element_type=F32
        )

    order = Plan(far, near).build()
    late = [unit for task in order if task[0] == "second" for unit in task[1:]][-LAST:]
    for task in order:
        kind = task[0]
        if kind in ("one", "two"):
            side = one if kind == "one" else two
            if task[1] == "far":
                side.take_far(*task[2:])
            else:
                side.take_near(*task[2:])
        elif kind == "first":
            first(*task[1:])
        elif kind == "mix":
            mix(*task[1:])
        elif kind == "sum":
            stage_sum(*task[1:])
        elif kind == "fresh":
            fresh(*task[1:])
        else:
            units = [unit for unit in task[1:] if unit not in late]
            for unit in units:
                two.ready(*unit)
            rows_bf = rows_of(next_cell, units) if units else None
            for j in range(tiles if units else 0):
                second(units, rows_bf, j)
    for unit in late:
        two.ready(*unit)
    late_rows = rows_of(next_cell, late)

    def balance(j):
        return jnp.mean(gene_bf[j].astype(F32), axis=1, keepdims=True)

    mine = lax.axis_index("cell")
    sum_copies = {}
    for j in range(tiles):
        second(late, late_rows, j)
        encode(acc[j] * balance(j), code.at[j], codem.at[j])
        for d in range(1, cells):
            where = {"cell": lax.rem(mine + d, cells)}
            send(code.at[j], other.at[mine, j], fs, fr.at[d - 1, j], where)
            send(codem.at[j], otherm.at[mine, j], uf, fr.at[d - 1, j], where)
        other[mine, j] = code[j]
        otherm[mine, j] = codem[j]
        if j == 0:
            drain(next_parts.at[pl.ds(0, group - 1)], nr.at[0])
            sums = jnp.sum(next_parts[...], axis=0)
            group_sum[...] = sums
            other_sum[mine] = sums
            for d in range(1, cells):
                sum_copies[d] = send(group_sum, other_sum.at[mine], os, orr.at[d - 1],
                                     {"cell": lax.rem(mine + d, cells)})
    for d in range(1, cells):
        sum_copies[d].wait_recv()
    sums = other_sum[0]
    for k in range(1, cells):
        sums += other_sum[k]
    for j in range(tiles):
        for d in range(1, cells):
            drain(size.at[pl.ds(0, width // 2 + 1)], fr.at[d - 1, j])
        value = decode(other.at[0, j], otherm.at[0, j])
        for k in range(1, cells):
            value += decode(other.at[k, j], otherm.at[k, j])
        gene_new[j] = gene[j] * (value / balance(j)) / sums
    one.close()
    two.close()
    drain(numer.at[0], s1)
    drain(t2.at[:, :, 0:near - 1], s2)
    drain(t2m.at[:, :, 0:near - 1], u2)
    drain(t3.at[:, 1:far], s3)
    drain(t3m.at[:, 1:far], u3)
    drain(parts.at[pl.ds(0, group - 1)], gs)
    drain(next_parts.at[pl.ds(0, group - 1)], ns)
    drain(other.at[0:cells - 1], fs)
    drain(otherm.at[0:cells - 1], uf)
    drain(other_sum.at[0:cells - 1], os)


VMEM = pl.BlockSpec(memory_space=pltpu.VMEM)
HBM = pl.BlockSpec(memory_space=pltpu.HBM)


def step(group, cells, blocks, brow, bcol, bcount, cell, gene):
    far, near, cores = digits(group)
    slots, width, _ = blocks.shape
    tiles, _, rank = gene.shape
    rows = cell.shape[0]
    prow = rows // PARTS
    spots = rows * group // width * tiles
    dma = pltpu.SemaphoreType.DMA
    vmem = pltpu.VMEM
    hke = (PARTS, far, near)
    return pl.pallas_call(
        functools.partial(step_kernel, group, cells),
        out_shape=(vmem(cell.shape, F32), vmem(gene.shape, F32)),
        in_specs=[HBM] * 6,
        out_specs=(VMEM, VMEM),
        scratch_shapes=[
            vmem((1, slots), I32),
            vmem((1, slots), I32),
            pltpu.SMEM((1,), I32),
            vmem((slots + 1, width, width), BF),
            vmem((spots, 128), I32),
            pltpu.SMEM((spots, 128), I32),
            vmem((rows, rank), F32),
            vmem((tiles, width, rank), F32),
            vmem((tiles, width, rank), BF),
            vmem((tiles, rank, width), BF),
            vmem((1, rank), F32),
            vmem((group, 1, rank), F32),
            vmem((PARTS, far * near, cores * prow, rank), BF),
            vmem((1, rank), F32),
            vmem((group, 1, rank), F32),
            vmem((PARTS, far * near, cores * prow, rank), BF),
            vmem((PARTS, far * near, cores * prow, rank), F32),
            vmem((*hke, prow, rank), F32),
            vmem((*hke, prow, rank), I16),
            vmem((PARTS, far, prow, rank), I16),
            vmem((*hke, prow, rank), I16),
            vmem((PARTS, far, prow, rank), I16),
            vmem((*hke, 1, rank), F32),
            vmem((PARTS, far, 1, rank), F32),
            vmem((*hke, 1, rank), F32),
            vmem((PARTS, far, 1, rank), F32),
            vmem((tiles, width, rank), F32),
            vmem((tiles, width, rank), I16),
            vmem((tiles, 1, rank), F32),
            vmem((cells, tiles, width, rank), I16),
            vmem((cells, tiles, 1, rank), F32),
            vmem((1, rank), F32),
            vmem((cells, 1, rank), F32),
            vmem((width // 2 + 1, 1, rank), F32),
        ] + gather_sems(far, near) + [dma((3,)), dma((10,)), dma(hke)]
        + [dma((PARTS, far, near - 1)), dma((PARTS, far - 1))] + [dma((1,))] * 2
        + [dma((cells - 1, tiles)), dma((cells - 1,)), dma((7,))],
        compiler_params=pltpu.CompilerParams(
            collective_id=0, has_side_effects=True, vmem_limit_bytes=60 * 1024 * 1024
        ),
        name="update_step",
    )(blocks, brow, bcol, bcount, cell, gene)


def on_device(cells, group, blocks, brow, bcol, bcount, cell_factor, gene_factor):
    _, width, _ = blocks.shape
    rank = cell_factor.shape[-1]
    tiles = gene_factor.shape[0] // width
    cell_new, gene_new = step(group, cells, blocks, brow.reshape(1, -1), bcol.reshape(1, -1), bcount,
                              cell_factor, gene_factor.reshape(tiles, width, rank))
    return cell_new, gene_new.reshape(gene_factor.shape)


def solution(mesh):
    sizes = dict(mesh.shape)
    placed = (
        P(("cell", "gene"), None, None),
        P(("cell", "gene")),
        P(("cell", "gene")),
        P(("cell", "gene")),
        P(("cell", "gene"), None),
        P("gene", None),
    )
    return jax.shard_map(
        functools.partial(on_device, sizes["cell"], sizes["gene"]),
        mesh=mesh,
        in_specs=placed,
        out_specs=(P(("cell", "gene"), None), P("gene", None)),
        check_vma=False,
    )
```

```python
import functools

import jax
import jax.numpy as jnp
from jax import lax
from jax.experimental import pallas as pl
from jax.experimental.pallas import tpu as pltpu
from jax.sharding import PartitionSpec as P

MESH = pl.DeviceIdType.MESH
F32 = jnp.float32
BF = jnp.bfloat16
I16 = jnp.int16
I32 = jnp.int32
CORES = 2
FAR = 4
PARTS = 2
LAST = 2
AHEAD = (1, 2, 3)
DIRECT = {"one": (), "sum": (), "two": ((0, 1), (1, 1))}
SPREAD = (3, 2, 1, 0)
PAIR = 0.5
COST = {"first": (1.24, 1.64), "second": (1.28, 1.8)}
WAIT = {"c": 0.95, "x": 1.8, "near": 2.6, "mid": 1.5}


def digits(group):
    return FAR, group // (FAR * CORES), CORES


def flip(v, k, n):
    if k == 0:
        return v
    if k == n - 1:
        return n - 1 - v
    if k == n // 2:
        return lax.rem(v + n // 2, n)
    return v + 1 - 2 * lax.rem(v, 2)


class Spot:
    def __init__(self, group):
        self.group = group
        self.far, self.near, self.cores = digits(group)
        self.me = lax.axis_index("gene")
        self.a = self.me // (self.near * self.cores)
        self.b = lax.rem(self.me // self.cores, self.near)
        self.c = lax.rem(self.me, self.cores)

    def unit(self, k, e):
        return flip(self.a, k, self.far) * self.near + flip(self.b, e, self.near)

    def peer(self, k, e, core):
        return {"gene": self.unit(k, e) * self.cores + core}


def send(src, dst, send_sem, recv_sem, where):
    copy = pltpu.make_async_remote_copy(
        src_ref=src, dst_ref=dst, send_sem=send_sem, recv_sem=recv_sem,
        device_id=where, device_id_type=MESH,
    )
    copy.start()
    return copy


def drain(ref, sem):
    pltpu.make_async_copy(ref, ref, sem).wait()


def greet(axis, size):
    barrier = pltpu.get_barrier_semaphore()
    me = lax.axis_index(axis)
    for d in range(1, size):
        pl.semaphore_signal(
            barrier, inc=1, device_id={axis: lax.rem(me + d, size)}, device_id_type=MESH
        )


def encode(value, code, scale):
    top = jnp.max(jnp.abs(value), axis=0, keepdims=True)
    factor = jnp.where(top > 0.0, 32767.0 / top, 0.0)
    code[...] = jnp.round(value * factor).astype(jnp.int32).astype(jnp.int16)
    scale[...] = top * (1.0 / 32767.0)


def decode(code, scale):
    return code[...].astype(jnp.int32).astype(F32) * scale[...]


class Gather:
    def __init__(self, spot, out, prow, direct, sems):
        self.direct = direct
        self.spot, self.out, self.prow = spot, out, prow
        self.sent, self.zr, self.xr, self.cr = sems
        self.zc, self.xc, self.cc = {}, {}, {}

    def place(self, h, k, e):
        spot = self.spot
        first = pl.multiple_of(spot.c * self.prow, self.prow)
        return self.out.at[h, spot.unit(k, e), pl.ds(first, self.prow)]

    def start(self, h):
        spot, src = self.spot, self.place(h, 0, 0)
        for k in AHEAD:
            self.zc[h, k] = send(src, src, self.sent.at[0], self.zr.at[h, k - 1],
                                 spot.peer(k, 0, spot.c))
        self.forward(h, 0)
        for k in AHEAD:
            for e in range(1, spot.near if (h, k) in self.direct else 1):
                self.xc[h, k, e] = send(src, src, self.sent.at[1], self.xr.at[h, k, e - 1],
                                        spot.peer(k, e, spot.c))

    def forward(self, h, k):
        spot, src = self.spot, self.place(h, k, 0)
        for e in range(1, 1 if (h, k) in self.direct else spot.near):
            self.xc[h, k, e] = send(src, src, self.sent.at[1], self.xr.at[h, k, e - 1],
                                    spot.peer(0, e, spot.c))
        self.pair(h, k, 0)

    def pair(self, h, k, e):
        spot, src = self.spot, self.place(h, k, e)
        self.cc[h, k, e] = send(src, src, self.sent.at[2], self.cr.at[h, k, e],
                                spot.peer(0, 0, 1 - spot.c))

    def take_far(self, h, k):
        self.zc[h, k].wait_recv()
        self.forward(h, k)

    def take_near(self, h, k, e):
        self.xc[h, k, e].wait_recv()
        self.pair(h, k, e)

    def ready(self, h, k, e):
        self.cc[h, k, e].wait_recv()

    def close(self):
        far, near = self.spot.far, self.spot.near
        for i, units in enumerate((far - 1, far * (near - 1), far * near)):
            drain(self.out.at[0, pl.ds(0, units)], self.sent.at[i])


def gather_sems(far, near):
    dma = pltpu.SemaphoreType.DMA
    return [dma((3,)), dma((PARTS, far - 1)), dma((PARTS, far, near - 1)), dma((PARTS, far, near))]


class Plan:
    def __init__(self, far, near):
        self.far, self.near = far, near
        self.time = 0.0
        self.free = {"c": 0.0, "x": 0.0, "near": 0.0, "mid": 0.0}
        self.arrive = {}
        self.order = []

    def post(self, key, k, e):
        link = ("x" if e else "c", "near", "mid", "mid")[k]
        wire = {"c": 0.1, "x": 1.4, "near": 1.4, "mid": 2.8}[link] / PARTS
        self.free[link] = max(self.time, self.free[link]) + wire
        self.arrive[key] = self.free[link] + WAIT[link] + (0.7 if k and e else 0.0)

    def begin(self, name, h):
        for k in AHEAD:
            self.post((name, "z", h, k), k, 0)
        self.ahead(name, h, 0)
        for k in AHEAD:
            for e in range(1, self.near if (h, k) in DIRECT[name] else 1):
                self.post((name, "x", h, k, e), k, e)

    def ahead(self, name, h, k):
        for e in range(1, 1 if (h, k) in DIRECT[name] else self.near):
            self.post((name, "x", h, k, e), 0, e)
        self.post((name, "c", h, k, 0), 0, 0)

    def tasks(self):
        far, near, parts = range(self.far), range(self.near), range(PARTS)
        mixed = [("p2", h, k, e) for h in parts for k in far for e in near[1:]]
        out = []
        for h in parts:
            out += [((name, "far", h, k), [(name, "z", h, k)], 0.02)
                    for name in ("one", "two") for k in far[1:]]
        for h in parts:
            need = [("p1", h, 0, 0)] + [("p3", h, k) for k in far[1:]]
            need += [key for key in mixed if key[1] == h and (key[2] == 0 or (h, key[2]) in DIRECT["sum"])]
            out.append((("fresh", h), need, 0.35))
        for h in parts:
            for k in reversed(far[1:]):
                need = [("p1", h, k, 0)]
                need += [key for key in mixed if key[1:3] == (h, k) and (h, k) not in DIRECT["sum"]]
                out.append((("sum", h, k), need, 0.15))
        for h in parts:
            out += [(("mix", h, k, e), [("p1", h, k, e)], 0.14)
                    for k in reversed(far) for e in near[1:]]
        for h in parts:
            out += [((name, "near", h, k, e), [(name, "x", h, k, e)], 0.02)
                    for name in ("one", "two") for k in far for e in near[1:]]
        spread = [(h, k, e) for h in parts for e in reversed(near) for k in SPREAD]
        for name, side in (("first", "one"), ("second", "two")):
            out += [((name, u), [(side, "c", *u)], COST[name][0] / PARTS) for u in spread]
        return out

    def run(self, task):
        kind = task[0]
        if kind == "first":
            for unit in task[1:]:
                self.post(("p1", *unit), 0, 0)
        elif kind == "mix":
            h, k, e = task[1:]
            self.post(("p2", h, k, e), k if (h, k) in DIRECT["sum"] else 0, e)
        elif kind == "sum":
            self.post(("p3", *task[1:]), task[2], 0)
        elif kind == "fresh":
            self.begin("two", task[1])
        elif kind in ("one", "two") and task[1] == "far":
            self.ahead(kind, task[2], task[3])
        elif kind in ("one", "two"):
            self.post((kind, "c", *task[2:]), 0, 0)

    def build(self):
        for h in range(PARTS):
            self.begin("one", h)
        self.time = 0.5
        left = self.tasks()
        while left:
            known = [(max(self.arrive[n] for n in need), i) for i, (_, need, _) in enumerate(left)
                     if all(n in self.arrive for n in need)]
            ready = [i for when, i in known if when <= self.time]
            if not ready:
                self.time = min(when for when, _ in known)
                continue
            pick = min(ready)
            kind = left[pick][0][0]
            if kind in COST:
                alike = sorted((max(when, self.time), i) for when, i in known
                               if left[i][0][0] == kind and i != pick)
                if alike and alike[0][0] <= self.time + PAIR:
                    self.time = alike[0][0]
                    other = alike[0][1]
                    units = left[pick][0][1:] + left[other][0][1:]
                    for i in sorted((pick, other), reverse=True):
                        left.pop(i)
                    left.insert(0, ((kind, *units), [], COST[kind][1] / PARTS))
                    pick = 0
            task, _, cost = left.pop(pick)
            self.time += cost
            self.run(task)
            self.order.append(task)
        return self.order


def step_kernel(group, cells, blocks, brow_in, bcol_in, bcount_in, cell_in, gene_in, cell_new,
                gene_new, brow, bcol, bcount, held, spread, table, cell, gene, gene_bf, flipped, own_sum, parts, cell_bf,
                next_sum, next_parts, next_cell, numer, p1, p2, p3, t2, t3,
                p2m, p3m, t2m, t3m, acc, code, codem, other, otherm, group_sum, other_sum, size, *sems):
    spot = Spot(group)
    far, near, cores = spot.far, spot.near, spot.cores
    c = spot.c
    slots, width, _ = blocks.shape
    tiles = gene.shape[0]
    rows = cell.shape[0]
    prow = rows // PARTS
    sub = width // rows
    one_sems, two_sems = sems[0:4], [sems[4], *sems[1:4]]
    sent, r1, r2, r3, gr, nr, fr, orr, ls = sems[5:]
    s1, s2, u2, s3, u3, gs, ns, fs, uf, os = (sent.at[i] for i in range(10))
    greet("gene", group)
    greet("cell", cells)
    load_cell = pltpu.make_async_copy(cell_in, cell, ls.at[0])
    load_cell.start()
    small = [pltpu.make_async_copy(src, dst, ls.at[4 + i])
             for i, (src, dst) in enumerate(((brow_in, brow), (bcol_in, bcol), (bcount_in, bcount)))]
    for copy in small:
        copy.start()
    load_gene = pltpu.make_async_copy(gene_in, gene, ls.at[1])
    load_gene.start()
    load = pltpu.make_async_copy(blocks, held.at[pl.ds(0, slots)], ls.at[2])
    load.start()

    held[slots] = jnp.zeros((width, width), BF)
    for copy in small:
        copy.wait()
    lane = lax.broadcasted_iota(I32, (1, slots), 1)
    where = jnp.where(lane < bcount[0], brow[...] * tiles + bcol[...], -1)
    at = lax.broadcasted_iota(I32, (spread.shape[0], slots), 0)
    found = jnp.min(jnp.where(at == where, lane, slots), axis=1, keepdims=True)
    spread[...] = jnp.broadcast_to(found, spread.shape)
    load_table = pltpu.make_async_copy(spread, table, ls.at[3])
    load_table.start()

    one = Gather(spot, cell_bf, prow, DIRECT["one"], one_sems)
    two = Gather(spot, next_cell, prow, DIRECT["two"], two_sems)
    load_cell.wait()
    for h in range(PARTS):
        one.place(h, 0, 0)[...] = cell[pl.ds(h * prow, prow), :].astype(BF)
    pl.semaphore_wait(pltpu.get_barrier_semaphore(), group - 1 + cells - 1)
    for h in range(PARTS):
        one.start(h)

    def share(src, out, ss, sr):
        for d in range(1, group):
            send(src, out.at[spot.me], ss, sr.at[0], {"gene": lax.rem(spot.me + d, group)})

    load_gene.wait()
    first_sum = jnp.zeros((1, gene.shape[-1]), F32)
    for j in range(tiles):
        first_sum += jnp.sum(gene[j], axis=0, keepdims=True)
    own_sum[...] = first_sum
    parts[spot.me] = first_sum
    share(own_sum, parts, gs, gr)
    for j in range(tiles):
        gene_bf[j] = gene[j].astype(BF)
        flipped[j] = gene[j].astype(BF).T
    acc[...] = jnp.zeros_like(acc)
    load_table.wait()
    load.wait()

    def rows_of(source, units):
        return jnp.concatenate([source[h, spot.unit(k, e)] for h, k, e in units], axis=0)

    def ratio_of(rows_bf, units, j):
        found = []
        for h, k, e in units:
            for core in range(cores):
                g = spot.unit(k, e) * cores + core
                slot = table[(g // sub) * tiles + j, 0]
                if sub == 1:
                    found.append(held[slot, pl.ds(h * prow, prow), :])
                else:
                    first = pl.multiple_of(lax.rem(g, sub) * rows + h * prow, prow)
                    found.append(held[slot, pl.ds(first, prow), :])
        x = jnp.concatenate(found, axis=0)
        model = jnp.dot(rows_bf, flipped[j], preferred_element_type=F32)
        return (x.astype(F32) / model).astype(BF)

    c1 = {}
    mine_at = pl.ds(pl.multiple_of(c * prow, prow), prow)
    theirs_at = pl.ds(pl.multiple_of((1 - c) * prow, prow), prow)

    def first(*units):
        for unit in units:
            one.ready(*unit)
        rows_bf = rows_of(cell_bf, units)
        total = None
        for j in range(tiles):
            ratio = ratio_of(rows_bf, units, j)
            term = jnp.dot(ratio, gene_bf[j], preferred_element_type=F32)
            total = term if total is None else total + term
        for i, (h, k, e) in enumerate(units):
            u = spot.unit(k, e)
            numer[h, u] = total[i * cores * prow:(i + 1) * cores * prow]
            c1[h, k, e] = send(numer.at[h, u, theirs_at], p1.at[h, k, e], s1,
                               r1.at[h, k, e], spot.peer(0, 0, 1 - c))

    def weight(h, u):
        return jnp.mean(cell_bf[h, u, mine_at].astype(F32), axis=1, keepdims=True)

    def both(h, k, e):
        c1[h, k, e].wait_recv()
        u = spot.unit(k, e)
        return (numer[h, u, mine_at] + p1[h, k, e]) * weight(h, u)

    def mix(h, k, e):
        encode(both(h, k, e), t2.at[h, k, e], t2m.at[h, k, e])
        where = spot.peer(k if (h, k) in DIRECT["sum"] else 0, e, c)
        send(t2.at[h, k, e], p2.at[h, k, e], s2, r2.at[h, k, e - 1], where)
        send(t2m.at[h, k, e], p2m.at[h, k, e], u2, r2.at[h, k, e - 1], where)

    def summed(h, k, mixed):
        value = both(h, k, 0)
        for i in mixed:
            for e in range(1, near):
                drain(size.at[pl.ds(0, prow // 2 + 1)], r2.at[h, i, e - 1])
                value += decode(p2.at[h, i, e], p2m.at[h, i, e])
        return value

    def stage_sum(h, k):
        encode(summed(h, k, () if (h, k) in DIRECT["sum"] else (k,)), t3.at[h, k], t3m.at[h, k])
        where = spot.peer(k, 0, c)
        send(t3.at[h, k], p3.at[h, k], s3, r3.at[h, k - 1], where)
        send(t3m.at[h, k], p3m.at[h, k], u3, r3.at[h, k - 1], where)

    sums_of = {}

    def fresh(h):
        if "total" not in sums_of:
            drain(parts.at[pl.ds(0, group - 1)], gr.at[0])
            sums_of["total"] = jnp.sum(parts[...], axis=0)
        value = summed(h, 0, [k for k in range(far) if k == 0 or (h, k) in DIRECT["sum"]])
        for k in range(1, far):
            drain(size.at[pl.ds(0, prow // 2 + 1)], r3.at[h, k - 1])
            value += decode(p3.at[h, k], p3m.at[h, k])
        value = value / weight(h, spot.unit(0, 0))
        new = cell[pl.ds(h * prow, prow), :] * value / sums_of["total"]
        two.place(h, 0, 0)[...] = new.astype(BF)
        two.start(h)
        cell_new[pl.ds(h * prow, prow), :] = new
        sums_of[h] = jnp.sum(new, axis=0, keepdims=True)
        if all(i in sums_of for i in range(PARTS)):
            total = sums_of[0]
            for i in range(1, PARTS):
                total = total + sums_of[i]
            next_sum[...] = total
            next_parts[spot.me] = total
            share(next_sum, next_parts, ns, nr)

    def second(units, rows_bf, j):
        ratio = ratio_of(rows_bf, units, j)
        acc[j] += lax.dot_general(
            ratio, rows_bf, (((0,), (0,)), ((), ())), preferred_element_type=F32
        )

    order = Plan(far, near).build()
    late = [unit for task in order if task[0] == "second" for unit in task[1:]][-LAST:]
    for task in order:
        kind = task[0]
        if kind in ("one", "two"):
            side = one if kind == "one" else two
            if task[1] == "far":
                side.take_far(*task[2:])
            else:
                side.take_near(*task[2:])
        elif kind == "first":
            first(*task[1:])
        elif kind == "mix":
            mix(*task[1:])
        elif kind == "sum":
            stage_sum(*task[1:])
        elif kind == "fresh":
            fresh(*task[1:])
        else:
            units = [unit for unit in task[1:] if unit not in late]
            for unit in units:
                two.ready(*unit)
            rows_bf = rows_of(next_cell, units) if units else None
            for j in range(tiles if units else 0):
                second(units, rows_bf, j)
    for unit in late:
        two.ready(*unit)
    late_rows = rows_of(next_cell, late)

    def balance(j):
        return jnp.mean(gene_bf[j].astype(F32), axis=1, keepdims=True)

    mine = lax.axis_index("cell")
    sum_copies = {}
    for j in range(tiles):
        second(late, late_rows, j)
        encode(acc[j] * balance(j), code.at[j], codem.at[j])
        for d in range(1, cells):
            where = {"cell": lax.rem(mine + d, cells)}
            send(code.at[j], other.at[mine, j], fs, fr.at[d - 1, j], where)
            send(codem.at[j], otherm.at[mine, j], uf, fr.at[d - 1, j], where)
        other[mine, j] = code[j]
        otherm[mine, j] = codem[j]
        if j == 0:
            drain(next_parts.at[pl.ds(0, group - 1)], nr.at[0])
            sums = jnp.sum(next_parts[...], axis=0)
            group_sum[...] = sums
            other_sum[mine] = sums
            for d in range(1, cells):
                sum_copies[d] = send(group_sum, other_sum.at[mine], os, orr.at[d - 1],
                                     {"cell": lax.rem(mine + d, cells)})
    for d in range(1, cells):
        sum_copies[d].wait_recv()
    sums = other_sum[0]
    for k in range(1, cells):
        sums += other_sum[k]
    for j in range(tiles):
        for d in range(1, cells):
            drain(size.at[pl.ds(0, width // 2 + 1)], fr.at[d - 1, j])
        value = decode(other.at[0, j], otherm.at[0, j])
        for k in range(1, cells):
            value += decode(other.at[k, j], otherm.at[k, j])
        gene_new[j] = gene[j] * (value / balance(j)) / sums
    one.close()
    two.close()
    drain(numer.at[0], s1)
    drain(t2.at[:, :, 0:near - 1], s2)
    drain(t2m.at[:, :, 0:near - 1], u2)
    drain(t3.at[:, 1:far], s3)
    drain(t3m.at[:, 1:far], u3)
    drain(parts.at[pl.ds(0, group - 1)], gs)
    drain(next_parts.at[pl.ds(0, group - 1)], ns)
    drain(other.at[0:cells - 1], fs)
    drain(otherm.at[0:cells - 1], uf)
    drain(other_sum.at[0:cells - 1], os)


VMEM = pl.BlockSpec(memory_space=pltpu.VMEM)
HBM = pl.BlockSpec(memory_space=pltpu.HBM)


def step(group, cells, blocks, brow, bcol, bcount, cell, gene):
    far, near, cores = digits(group)
    slots, width, _ = blocks.shape
    tiles, _, rank = gene.shape
    rows = cell.shape[0]
    prow = rows // PARTS
    spots = rows * group // width * tiles
    dma = pltpu.SemaphoreType.DMA
    vmem = pltpu.VMEM
    hke = (PARTS, far, near)
    return pl.pallas_call(
        functools.partial(step_kernel, group, cells),
        out_shape=(vmem(cell.shape, F32), vmem(gene.shape, F32)),
        in_specs=[HBM] * 6,
        out_specs=(VMEM, VMEM),
        scratch_shapes=[
            vmem((1, slots), I32),
            vmem((1, slots), I32),
            pltpu.SMEM((1,), I32),
            vmem((slots + 1, width, width), BF),
            vmem((spots, 128), I32),
            pltpu.SMEM((spots, 128), I32),
            vmem((rows, rank), F32),
            vmem((tiles, width, rank), F32),
            vmem((tiles, width, rank), BF),
            vmem((tiles, rank, width), BF),
            vmem((1, rank), F32),
            vmem((group, 1, rank), F32),
            vmem((PARTS, far * near, cores * prow, rank), BF),
            vmem((1, rank), F32),
            vmem((group, 1, rank), F32),
            vmem((PARTS, far * near, cores * prow, rank), BF),
            vmem((PARTS, far * near, cores * prow, rank), F32),
            vmem((*hke, prow, rank), F32),
            vmem((*hke, prow, rank), I16),
            vmem((PARTS, far, prow, rank), I16),
            vmem((*hke, prow, rank), I16),
            vmem((PARTS, far, prow, rank), I16),
            vmem((*hke, 1, rank), F32),
            vmem((PARTS, far, 1, rank), F32),
            vmem((*hke, 1, rank), F32),
            vmem((PARTS, far, 1, rank), F32),
            vmem((tiles, width, rank), F32),
            vmem((tiles, width, rank), I16),
            vmem((tiles, 1, rank), F32),
            vmem((cells, tiles, width, rank), I16),
            vmem((cells, tiles, 1, rank), F32),
            vmem((1, rank), F32),
            vmem((cells, 1, rank), F32),
            vmem((width // 2 + 1, 1, rank), F32),
        ] + gather_sems(far, near) + [dma((3,)), dma((10,)), dma(hke)]
        + [dma((PARTS, far, near - 1)), dma((PARTS, far - 1))] + [dma((1,))] * 2
        + [dma((cells - 1, tiles)), dma((cells - 1,)), dma((7,))],
        compiler_params=pltpu.CompilerParams(
            collective_id=0, has_side_effects=True, vmem_limit_bytes=60 * 1024 * 1024
        ),
        name="update_step",
    )(blocks, brow, bcol, bcount, cell, gene)


def on_device(cells, group, blocks, brow, bcol, bcount, cell_factor, gene_factor):
    _, width, _ = blocks.shape
    rank = cell_factor.shape[-1]
    tiles = gene_factor.shape[0] // width
    cell_new, gene_new = step(group, cells, blocks, brow.reshape(1, -1), bcol.reshape(1, -1), bcount,
                              cell_factor, gene_factor.reshape(tiles, width, rank))
    return cell_new, gene_new.reshape(gene_factor.shape)


def solution(mesh):
    sizes = dict(mesh.shape)
    placed = (
        P(("cell", "gene"), None, None),
        P(("cell", "gene")),
        P(("cell", "gene")),
        P(("cell", "gene")),
        P(("cell", "gene"), None),
        P("gene", None),
    )
    return jax.shard_map(
        functools.partial(on_device, sizes["cell"], sizes["gene"]),
        mesh=mesh,
        in_specs=placed,
        out_specs=(P(("cell", "gene"), None), P("gene", None)),
        check_vma=False,
    )
```

```python
import functools

import jax
import jax.numpy as jnp
from jax import lax
from jax.experimental import pallas as pl
from jax.experimental.pallas import tpu as pltpu
from jax.sharding import PartitionSpec as P

MESH = pl.DeviceIdType.MESH
F32 = jnp.float32
BF = jnp.bfloat16
I16 = jnp.int16
I32 = jnp.int32
CORES = 2
FAR = 4
PARTS = 2
LAST = 2
AHEAD = (1, 2, 3)
DIRECT = {"one": (), "sum": (), "two": ((0, 1), (1, 1))}
SPREAD = (3, 2, 0, 1)
PAIR = 0.5
COST = {"first": (1.24, 1.64), "second": (1.28, 1.8)}
WAIT = {"c": 0.95, "x": 1.8, "near": 2.6, "mid": 1.5}


def digits(group):
    return FAR, group // (FAR * CORES), CORES


def flip(v, k, n):
    if k == 0:
        return v
    if k == n - 1:
        return n - 1 - v
    if k == n // 2:
        return lax.rem(v + n // 2, n)
    return v + 1 - 2 * lax.rem(v, 2)


class Spot:
    def __init__(self, group):
        self.group = group
        self.far, self.near, self.cores = digits(group)
        self.me = lax.axis_index("gene")
        self.a = self.me // (self.near * self.cores)
        self.b = lax.rem(self.me // self.cores, self.near)
        self.c = lax.rem(self.me, self.cores)

    def unit(self, k, e):
        return flip(self.a, k, self.far) * self.near + flip(self.b, e, self.near)

    def peer(self, k, e, core):
        return {"gene": self.unit(k, e) * self.cores + core}


def send(src, dst, send_sem, recv_sem, where):
    copy = pltpu.make_async_remote_copy(
        src_ref=src, dst_ref=dst, send_sem=send_sem, recv_sem=recv_sem,
        device_id=where, device_id_type=MESH,
    )
    copy.start()
    return copy


def drain(ref, sem):
    pltpu.make_async_copy(ref, ref, sem).wait()


def greet(axis, size):
    barrier = pltpu.get_barrier_semaphore()
    me = lax.axis_index(axis)
    for d in range(1, size):
        pl.semaphore_signal(
            barrier, inc=1, device_id={axis: lax.rem(me + d, size)}, device_id_type=MESH
        )


def encode(value, code, scale):
    top = jnp.max(jnp.abs(value), axis=0, keepdims=True)
    factor = jnp.where(top > 0.0, 32767.0 / top, 0.0)
    code[...] = jnp.round(value * factor).astype(jnp.int32).astype(jnp.int16)
    scale[...] = top * (1.0 / 32767.0)


def decode(code, scale):
    return code[...].astype(jnp.int32).astype(F32) * scale[...]


class Gather:
    def __init__(self, spot, out, prow, direct, sems):
        self.direct = direct
        self.spot, self.out, self.prow = spot, out, prow
        self.sent, self.zr, self.xr, self.cr = sems
        self.zc, self.xc, self.cc = {}, {}, {}

    def place(self, h, k, e):
        spot = self.spot
        first = pl.multiple_of(spot.c * self.prow, self.prow)
        return self.out.at[h, spot.unit(k, e), pl.ds(first, self.prow)]

    def start(self, h):
        spot, src = self.spot, self.place(h, 0, 0)
        self.forward(h, 0)
        for k in AHEAD:
            self.zc[h, k] = send(src, src, self.sent.at[0], self.zr.at[h, k - 1],
                                 spot.peer(k, 0, spot.c))
        for k in AHEAD:
            for e in range(1, spot.near if (h, k) in self.direct else 1):
                self.xc[h, k, e] = send(src, src, self.sent.at[1], self.xr.at[h, k, e - 1],
                                        spot.peer(k, e, spot.c))

    def forward(self, h, k):
        spot, src = self.spot, self.place(h, k, 0)
        for e in range(1, 1 if (h, k) in self.direct else spot.near):
            self.xc[h, k, e] = send(src, src, self.sent.at[1], self.xr.at[h, k, e - 1],
                                    spot.peer(0, e, spot.c))
        self.pair(h, k, 0)

    def pair(self, h, k, e):
        spot, src = self.spot, self.place(h, k, e)
        self.cc[h, k, e] = send(src, src, self.sent.at[2], self.cr.at[h, k, e],
                                spot.peer(0, 0, 1 - spot.c))

    def take_far(self, h, k):
        self.zc[h, k].wait_recv()
        self.forward(h, k)

    def take_near(self, h, k, e):
        self.xc[h, k, e].wait_recv()
        self.pair(h, k, e)

    def ready(self, h, k, e):
        self.cc[h, k, e].wait_recv()

    def close(self):
        far, near = self.spot.far, self.spot.near
        for i, units in enumerate((far - 1, far * (near - 1), far * near)):
            drain(self.out.at[0, pl.ds(0, units)], self.sent.at[i])


def gather_sems(far, near):
    dma = pltpu.SemaphoreType.DMA
    return [dma((3,)), dma((PARTS, far - 1)), dma((PARTS, far, near - 1)), dma((PARTS, far, near))]


class Plan:
    def __init__(self, far, near):
        self.far, self.near = far, near
        self.time = 0.0
        self.free = {"c": 0.0, "x": 0.0, "near": 0.0, "mid": 0.0}
        self.arrive = {}
        self.order = []

    def post(self, key, k, e):
        link = ("x" if e else "c", "near", "mid", "mid")[k]
        wire = {"c": 0.1, "x": 1.4, "near": 1.4, "mid": 2.8}[link] / PARTS
        self.free[link] = max(self.time, self.free[link]) + wire
        self.arrive[key] = self.free[link] + WAIT[link] + (0.7 if k and e else 0.0)

    def begin(self, name, h):
        for k in AHEAD:
            self.post((name, "z", h, k), k, 0)
        self.ahead(name, h, 0)
        for k in AHEAD:
            for e in range(1, self.near if (h, k) in DIRECT[name] else 1):
                self.post((name, "x", h, k, e), k, e)

    def ahead(self, name, h, k):
        for e in range(1, 1 if (h, k) in DIRECT[name] else self.near):
            self.post((name, "x", h, k, e), 0, e)
        self.post((name, "c", h, k, 0), 0, 0)

    def tasks(self):
        far, near, parts = range(self.far), range(self.near), range(PARTS)
        mixed = [("p2", h, k, e) for h in parts for k in far for e in near[1:]]
        out = []
        for h in parts:
            out += [((name, "far", h, k), [(name, "z", h, k)], 0.02)
                    for name in ("one", "two") for k in far[1:]]
        for h in parts:
            need = [("p1", h, 0, 0)] + [("p3", h, k) for k in far[1:]]
            need += [key for key in mixed if key[1] == h and (key[2] == 0 or (h, key[2]) in DIRECT["sum"])]
            out.append((("fresh", h), need, 0.35))
        for h in parts:
            for k in reversed(far[1:]):
                need = [("p1", h, k, 0)]
                need += [key for key in mixed if key[1:3] == (h, k) and (h, k) not in DIRECT["sum"]]
                out.append((("sum", h, k), need, 0.15))
        for h in parts:
            out += [(("mix", h, k, e), [("p1", h, k, e)], 0.14)
                    for k in reversed(far) for e in near[1:]]
        for h in parts:
            out += [((name, "near", h, k, e), [(name, "x", h, k, e)], 0.02)
                    for name in ("one", "two") for k in far for e in near[1:]]
        spread = [(h, k, e) for h in parts for e in reversed(near) for k in SPREAD]
        for name, side in (("first", "one"), ("second", "two")):
            out += [((name, u), [(side, "c", *u)], COST[name][0] / PARTS) for u in spread]
        return out

    def run(self, task):
        kind = task[0]
        if kind == "first":
            for unit in task[1:]:
                self.post(("p1", *unit), 0, 0)
        elif kind == "mix":
            h, k, e = task[1:]
            self.post(("p2", h, k, e), k if (h, k) in DIRECT["sum"] else 0, e)
        elif kind == "sum":
            self.post(("p3", *task[1:]), task[2], 0)
        elif kind == "fresh":
            self.begin("two", task[1])
        elif kind in ("one", "two") and task[1] == "far":
            self.ahead(kind, task[2], task[3])
        elif kind in ("one", "two"):
            self.post((kind, "c", *task[2:]), 0, 0)

    def build(self):
        for h in range(PARTS):
            self.begin("one", h)
        self.time = 0.5
        left = self.tasks()
        while left:
            known = [(max(self.arrive[n] for n in need), i) for i, (_, need, _) in enumerate(left)
                     if all(n in self.arrive for n in need)]
            ready = [i for when, i in known if when <= self.time]
            if not ready:
                self.time = min(when for when, _ in known)
                continue
            pick = min(ready)
            kind = left[pick][0][0]
            if kind in COST:
                alike = sorted((max(when, self.time), i) for when, i in known
                               if left[i][0][0] == kind and i != pick)
                if alike and alike[0][0] <= self.time + PAIR:
                    self.time = alike[0][0]
                    other = alike[0][1]
                    units = left[pick][0][1:] + left[other][0][1:]
                    for i in sorted((pick, other), reverse=True):
                        left.pop(i)
                    left.insert(0, ((kind, *units), [], COST[kind][1] / PARTS))
                    pick = 0
            task, _, cost = left.pop(pick)
            self.time += cost
            self.run(task)
            self.order.append(task)
        return self.order


def step_kernel(group, cells, blocks, brow_in, bcol_in, bcount_in, cell_in, gene_in, cell_new,
                gene_new, brow, bcol, bcount, held, spread, table, cell, gene, gene_bf, flipped, own_sum, parts, cell_bf,
                next_sum, next_parts, next_cell, numer, p1, p2, p3, t2, t3,
                p2m, p3m, t2m, t3m, acc, code, codem, other, otherm, group_sum, other_sum, size, even, *sems):
    spot = Spot(group)
    far, near, cores = spot.far, spot.near, spot.cores
    c = spot.c
    slots, width, _ = blocks.shape
    tiles = gene.shape[0]
    rows = cell.shape[0]
    prow = rows // PARTS
    sub = width // rows
    one_sems, two_sems = sems[0:4], [sems[4], *sems[1:4]]
    sent, r1, r2, r3, gr, nr, fr, orr, ls = sems[5:]
    s1, s2, u2, s3, u3, gs, ns, fs, uf, os = (sent.at[i] for i in range(10))
    greet("gene", group)
    greet("cell", cells)
    load_cell = pltpu.make_async_copy(cell_in, cell, ls.at[0])
    load_cell.start()
    small = [pltpu.make_async_copy(src, dst, ls.at[4 + i])
             for i, (src, dst) in enumerate(((brow_in, brow), (bcol_in, bcol), (bcount_in, bcount)))]
    for copy in small:
        copy.start()
    load_gene = pltpu.make_async_copy(gene_in, gene, ls.at[1])
    load_gene.start()
    load = pltpu.make_async_copy(blocks, held.at[pl.ds(0, slots)], ls.at[2])
    load.start()

    one = Gather(spot, cell_bf, prow, DIRECT["one"], one_sems)
    two = Gather(spot, next_cell, prow, DIRECT["two"], two_sems)
    load_cell.wait()
    for h in range(PARTS):
        one.place(h, 0, 0)[...] = cell[pl.ds(h * prow, prow), :].astype(BF)
    pl.semaphore_wait(pltpu.get_barrier_semaphore(), group - 1 + cells - 1)
    for h in range(PARTS):
        one.start(h)

    held[slots] = jnp.zeros((width, width), BF)
    for copy in small:
        copy.wait()
    lane = lax.broadcasted_iota(I32, (1, slots), 1)
    where = jnp.where(lane < bcount[0], brow[...] * tiles + bcol[...], -1)
    at = lax.broadcasted_iota(I32, (spread.shape[0], slots), 0)
    found = jnp.min(jnp.where(at == where, lane, slots), axis=1, keepdims=True)
    spread[...] = jnp.broadcast_to(found, spread.shape)
    load_table = pltpu.make_async_copy(spread, table, ls.at[3])
    load_table.start()

    def share(src, out, ss, sr):
        for d in range(1, group):
            send(src, out.at[spot.me], ss, sr.at[0], {"gene": lax.rem(spot.me + d, group)})

    load_gene.wait()
    first_sum = jnp.zeros((1, gene.shape[-1]), F32)
    for j in range(tiles):
        first_sum += jnp.sum(gene[j], axis=0, keepdims=True)
    own_sum[...] = first_sum
    parts[spot.me] = first_sum
    share(own_sum, parts, gs, gr)
    for j in range(tiles):
        gene_bf[j] = gene[j].astype(BF)
        flipped[j] = gene[j].astype(BF).T
        mean = jnp.mean(gene[j].astype(BF).astype(F32), axis=1, keepdims=True)
        even[j] = jnp.broadcast_to(mean, even.shape[1:])
    acc[...] = jnp.zeros_like(acc)
    load_table.wait()
    load.wait()

    def rows_of(source, units):
        return jnp.concatenate([source[h, spot.unit(k, e)] for h, k, e in units], axis=0)

    def ratio_of(rows_bf, units, j):
        found = []
        for h, k, e in units:
            for core in range(cores):
                g = spot.unit(k, e) * cores + core
                slot = table[(g // sub) * tiles + j, 0]
                if sub == 1:
                    found.append(held[slot, pl.ds(h * prow, prow), :])
                else:
                    first = pl.multiple_of(lax.rem(g, sub) * rows + h * prow, prow)
                    found.append(held[slot, pl.ds(first, prow), :])
        x = jnp.concatenate(found, axis=0)
        model = jnp.dot(rows_bf, flipped[j], preferred_element_type=F32)
        return (x.astype(F32) / model).astype(BF)

    c1 = {}
    mine_at = pl.ds(pl.multiple_of(c * prow, prow), prow)
    theirs_at = pl.ds(pl.multiple_of((1 - c) * prow, prow), prow)

    def first(*units):
        for unit in units:
            one.ready(*unit)
        rows_bf = rows_of(cell_bf, units)
        total = None
        for j in range(tiles):
            ratio = ratio_of(rows_bf, units, j)
            term = jnp.dot(ratio, gene_bf[j], preferred_element_type=F32)
            total = term if total is None else total + term
        for i, (h, k, e) in enumerate(units):
            u = spot.unit(k, e)
            numer[h, u] = total[i * cores * prow:(i + 1) * cores * prow]
            c1[h, k, e] = send(numer.at[h, u, theirs_at], p1.at[h, k, e], s1,
                               r1.at[h, k, e], spot.peer(0, 0, 1 - c))

    def weight(h, u):
        return jnp.mean(cell_bf[h, u, mine_at].astype(F32), axis=1, keepdims=True)

    def both(h, k, e):
        c1[h, k, e].wait_recv()
        u = spot.unit(k, e)
        return (numer[h, u, mine_at] + p1[h, k, e]) * weight(h, u)

    def mix(h, k, e):
        encode(both(h, k, e), t2.at[h, k, e], t2m.at[h, k, e])
        where = spot.peer(k if (h, k) in DIRECT["sum"] else 0, e, c)
        send(t2.at[h, k, e], p2.at[h, k, e], s2, r2.at[h, k, e - 1], where)
        send(t2m.at[h, k, e], p2m.at[h, k, e], u2, r2.at[h, k, e - 1], where)

    def summed(h, k, mixed):
        value = both(h, k, 0)
        for i in mixed:
            for e in range(1, near):
                drain(size.at[pl.ds(0, prow // 2 + 1)], r2.at[h, i, e - 1])
                value += decode(p2.at[h, i, e], p2m.at[h, i, e])
        return value

    def stage_sum(h, k):
        encode(summed(h, k, () if (h, k) in DIRECT["sum"] else (k,)), t3.at[h, k], t3m.at[h, k])
        where = spot.peer(k, 0, c)
        send(t3.at[h, k], p3.at[h, k], s3, r3.at[h, k - 1], where)
        send(t3m.at[h, k], p3m.at[h, k], u3, r3.at[h, k - 1], where)

    sums_of = {}

    def fresh(h):
        if "total" not in sums_of:
            drain(parts.at[pl.ds(0, group - 1)], gr.at[0])
            sums_of["total"] = jnp.sum(parts[...], axis=0)
        value = summed(h, 0, [k for k in range(far) if k == 0 or (h, k) in DIRECT["sum"]])
        for k in range(1, far):
            drain(size.at[pl.ds(0, prow // 2 + 1)], r3.at[h, k - 1])
            value += decode(p3.at[h, k], p3m.at[h, k])
        value = value / weight(h, spot.unit(0, 0))
        new = cell[pl.ds(h * prow, prow), :] * value / sums_of["total"]
        two.place(h, 0, 0)[...] = new.astype(BF)
        two.start(h)
        cell_new[pl.ds(h * prow, prow), :] = new
        sums_of[h] = jnp.sum(new, axis=0, keepdims=True)
        if all(i in sums_of for i in range(PARTS)):
            total = sums_of[0]
            for i in range(1, PARTS):
                total = total + sums_of[i]
            next_sum[...] = total
            next_parts[spot.me] = total
            share(next_sum, next_parts, ns, nr)

    def second(units, rows_bf, j):
        ratio = ratio_of(rows_bf, units, j)
        acc[j] += lax.dot_general(
            ratio, rows_bf, (((0,), (0,)), ((), ())), preferred_element_type=F32
        )

    order = Plan(far, near).build()
    late = [unit for task in order if task[0] == "second" for unit in task[1:]][-LAST:]
    for task in order:
        kind = task[0]
        if kind in ("one", "two"):
            side = one if kind == "one" else two
            if task[1] == "far":
                side.take_far(*task[2:])
            else:
                side.take_near(*task[2:])
        elif kind == "first":
            first(*task[1:])
        elif kind == "mix":
            mix(*task[1:])
        elif kind == "sum":
            stage_sum(*task[1:])
        elif kind == "fresh":
            fresh(*task[1:])
        else:
            units = [unit for unit in task[1:] if unit not in late]
            for unit in units:
                two.ready(*unit)
            rows_bf = rows_of(next_cell, units) if units else None
            for j in range(tiles if units else 0):
                second(units, rows_bf, j)
    for unit in late:
        two.ready(*unit)
    late_rows = rows_of(next_cell, late)

    def balance(j):
        return even[j]

    mine = lax.axis_index("cell")
    sum_copies = {}
    for j in range(tiles):
        second(late, late_rows, j)
        encode(acc[j] * balance(j), code.at[j], codem.at[j])
        for d in range(1, cells):
            where = {"cell": lax.rem(mine + d, cells)}
            send(code.at[j], other.at[mine, j], fs, fr.at[d - 1, j], where)
            send(codem.at[j], otherm.at[mine, j], uf, fr.at[d - 1, j], where)
        other[mine, j] = code[j]
        otherm[mine, j] = codem[j]
        if j == 0:
            drain(next_parts.at[pl.ds(0, group - 1)], nr.at[0])
            sums = jnp.sum(next_parts[...], axis=0)
            group_sum[...] = sums
            other_sum[mine] = sums
            for d in range(1, cells):
                sum_copies[d] = send(group_sum, other_sum.at[mine], os, orr.at[d - 1],
                                     {"cell": lax.rem(mine + d, cells)})
    for d in range(1, cells):
        sum_copies[d].wait_recv()
    sums = other_sum[0]
    for k in range(1, cells):
        sums += other_sum[k]
    for j in range(tiles):
        for d in range(1, cells):
            drain(size.at[pl.ds(0, width // 2 + 1)], fr.at[d - 1, j])
        value = decode(other.at[0, j], otherm.at[0, j])
        for k in range(1, cells):
            value += decode(other.at[k, j], otherm.at[k, j])
        gene_new[j] = gene[j] * (value / even[j]) / sums
    one.close()
    two.close()
    drain(numer.at[0], s1)
    drain(t2.at[:, :, 0:near - 1], s2)
    drain(t2m.at[:, :, 0:near - 1], u2)
    drain(t3.at[:, 1:far], s3)
    drain(t3m.at[:, 1:far], u3)
    drain(parts.at[pl.ds(0, group - 1)], gs)
    drain(next_parts.at[pl.ds(0, group - 1)], ns)
    drain(other.at[0:cells - 1], fs)
    drain(otherm.at[0:cells - 1], uf)
    drain(other_sum.at[0:cells - 1], os)


VMEM = pl.BlockSpec(memory_space=pltpu.VMEM)
HBM = pl.BlockSpec(memory_space=pltpu.HBM)


def step(group, cells, blocks, brow, bcol, bcount, cell, gene):
    far, near, cores = digits(group)
    slots, width, _ = blocks.shape
    tiles, _, rank = gene.shape
    rows = cell.shape[0]
    prow = rows // PARTS
    spots = rows * group // width * tiles
    dma = pltpu.SemaphoreType.DMA
    vmem = pltpu.VMEM
    hke = (PARTS, far, near)
    return pl.pallas_call(
        functools.partial(step_kernel, group, cells),
        out_shape=(vmem(cell.shape, F32), vmem(gene.shape, F32)),
        in_specs=[HBM] * 6,
        out_specs=(VMEM, VMEM),
        scratch_shapes=[
            vmem((1, slots), I32),
            vmem((1, slots), I32),
            pltpu.SMEM((1,), I32),
            vmem((slots + 1, width, width), BF),
            vmem((spots, 128), I32),
            pltpu.SMEM((spots, 128), I32),
            vmem((rows, rank), F32),
            vmem((tiles, width, rank), F32),
            vmem((tiles, width, rank), BF),
            vmem((tiles, rank, width), BF),
            vmem((1, rank), F32),
            vmem((group, 1, rank), F32),
            vmem((PARTS, far * near, cores * prow, rank), BF),
            vmem((1, rank), F32),
            vmem((group, 1, rank), F32),
            vmem((PARTS, far * near, cores * prow, rank), BF),
            vmem((PARTS, far * near, cores * prow, rank), F32),
            vmem((*hke, prow, rank), F32),
            vmem((*hke, prow, rank), I16),
            vmem((PARTS, far, prow, rank), I16),
            vmem((*hke, prow, rank), I16),
            vmem((PARTS, far, prow, rank), I16),
            vmem((*hke, 1, rank), F32),
            vmem((PARTS, far, 1, rank), F32),
            vmem((*hke, 1, rank), F32),
            vmem((PARTS, far, 1, rank), F32),
            vmem((tiles, width, rank), F32),
            vmem((tiles, width, rank), I16),
            vmem((tiles, 1, rank), F32),
            vmem((cells, tiles, width, rank), I16),
            vmem((cells, tiles, 1, rank), F32),
            vmem((1, rank), F32),
            vmem((cells, 1, rank), F32),
            vmem((width // 2 + 1, 1, rank), F32),
            vmem((tiles, width, rank), F32),
        ] + gather_sems(far, near) + [dma((3,)), dma((10,)), dma(hke)]
        + [dma((PARTS, far, near - 1)), dma((PARTS, far - 1))] + [dma((1,))] * 2
        + [dma((cells - 1, tiles)), dma((cells - 1,)), dma((7,))],
        compiler_params=pltpu.CompilerParams(
            collective_id=0, has_side_effects=True, vmem_limit_bytes=60 * 1024 * 1024
        ),
        name="update_step",
    )(blocks, brow, bcol, bcount, cell, gene)


def on_device(cells, group, blocks, brow, bcol, bcount, cell_factor, gene_factor):
    _, width, _ = blocks.shape
    rank = cell_factor.shape[-1]
    tiles = gene_factor.shape[0] // width
    cell_new, gene_new = step(group, cells, blocks, brow.reshape(1, -1), bcol.reshape(1, -1), bcount,
                              cell_factor, gene_factor.reshape(tiles, width, rank))
    return cell_new, gene_new.reshape(gene_factor.shape)


def solution(mesh):
    sizes = dict(mesh.shape)
    placed = (
        P(("cell", "gene"), None, None),
        P(("cell", "gene")),
        P(("cell", "gene")),
        P(("cell", "gene")),
        P(("cell", "gene"), None),
        P("gene", None),
    )
    return jax.shard_map(
        functools.partial(on_device, sizes["cell"], sizes["gene"]),
        mesh=mesh,
        in_specs=placed,
        out_specs=(P(("cell", "gene"), None), P("gene", None)),
        check_vma=False,
    )
```

```python
import functools

import jax
import jax.numpy as jnp
from jax import lax
from jax.experimental import pallas as pl
from jax.experimental.pallas import tpu as pltpu
from jax.sharding import PartitionSpec as P

MESH = pl.DeviceIdType.MESH
F32 = jnp.float32
BF = jnp.bfloat16
I16 = jnp.int16
I32 = jnp.int32
CORES = 2
FAR = 4
PARTS = 2
LAST = 2
AHEAD = (1, 2, 3)
DIRECT = {"one": (), "sum": (), "two": ((0, 1), (1, 1))}
SPREAD = (2, 3, 1, 0)
PAIR = 0.5
COST = {"first": (1.24, 1.64), "second": (1.28, 1.8)}
WAIT = {"c": 0.95, "x": 1.8, "near": 2.6, "mid": 1.5}


def digits(group):
    return FAR, group // (FAR * CORES), CORES


def flip(v, k, n):
    if k == 0:
        return v
    if k == n - 1:
        return n - 1 - v
    if k == n // 2:
        return lax.rem(v + n // 2, n)
    return v + 1 - 2 * lax.rem(v, 2)


class Spot:
    def __init__(self, group):
        self.group = group
        self.far, self.near, self.cores = digits(group)
        self.me = lax.axis_index("gene")
        self.a = self.me // (self.near * self.cores)
        self.b = lax.rem(self.me // self.cores, self.near)
        self.c = lax.rem(self.me, self.cores)

    def unit(self, k, e):
        return flip(self.a, k, self.far) * self.near + flip(self.b, e, self.near)

    def peer(self, k, e, core):
        return {"gene": self.unit(k, e) * self.cores + core}


def send(src, dst, send_sem, recv_sem, where):
    copy = pltpu.make_async_remote_copy(
        src_ref=src, dst_ref=dst, send_sem=send_sem, recv_sem=recv_sem,
        device_id=where, device_id_type=MESH,
    )
    copy.start()
    return copy


def drain(ref, sem):
    pltpu.make_async_copy(ref, ref, sem).wait()


def greet(axis, size):
    barrier = pltpu.get_barrier_semaphore()
    me = lax.axis_index(axis)
    for d in range(1, size):
        pl.semaphore_signal(
            barrier, inc=1, device_id={axis: lax.rem(me + d, size)}, device_id_type=MESH
        )


def encode(value, code, scale):
    top = jnp.max(jnp.abs(value), axis=0, keepdims=True)
    factor = jnp.where(top > 0.0, 32767.0 / top, 0.0)
    code[...] = jnp.round(value * factor).astype(jnp.int32).astype(jnp.int16)
    scale[...] = top * (1.0 / 32767.0)


def decode(code, scale):
    return code[...].astype(jnp.int32).astype(F32) * scale[...]


class Gather:
    def __init__(self, spot, out, prow, direct, sems):
        self.direct = direct
        self.spot, self.out, self.prow = spot, out, prow
        self.sent, self.zr, self.xr, self.cr = sems
        self.zc, self.xc, self.cc = {}, {}, {}

    def place(self, h, k, e):
        spot = self.spot
        first = pl.multiple_of(spot.c * self.prow, self.prow)
        return self.out.at[h, spot.unit(k, e), pl.ds(first, self.prow)]

    def start(self, h):
        spot, src = self.spot, self.place(h, 0, 0)
        self.forward(h, 0)
        for k in AHEAD:
            self.zc[h, k] = send(src, src, self.sent.at[0], self.zr.at[h, k - 1],
                                 spot.peer(k, 0, spot.c))
        for k in AHEAD:
            for e in range(1, spot.near if (h, k) in self.direct else 1):
                self.xc[h, k, e] = send(src, src, self.sent.at[1], self.xr.at[h, k, e - 1],
                                        spot.peer(k, e, spot.c))

    def forward(self, h, k):
        spot, src = self.spot, self.place(h, k, 0)
        for e in range(1, 1 if (h, k) in self.direct else spot.near):
            self.xc[h, k, e] = send(src, src, self.sent.at[1], self.xr.at[h, k, e - 1],
                                    spot.peer(0, e, spot.c))
        self.pair(h, k, 0)

    def pair(self, h, k, e):
        spot, src = self.spot, self.place(h, k, e)
        self.cc[h, k, e] = send(src, src, self.sent.at[2], self.cr.at[h, k, e],
                                spot.peer(0, 0, 1 - spot.c))

    def take_far(self, h, k):
        self.zc[h, k].wait_recv()
        self.forward(h, k)

    def take_near(self, h, k, e):
        self.xc[h, k, e].wait_recv()
        self.pair(h, k, e)

    def ready(self, h, k, e):
        self.cc[h, k, e].wait_recv()

    def close(self):
        far, near = self.spot.far, self.spot.near
        for i, units in enumerate((far - 1, far * (near - 1), far * near)):
            drain(self.out.at[0, pl.ds(0, units)], self.sent.at[i])


def gather_sems(far, near):
    dma = pltpu.SemaphoreType.DMA
    return [dma((3,)), dma((PARTS, far - 1)), dma((PARTS, far, near - 1)), dma((PARTS, far, near))]


class Plan:
    def __init__(self, far, near):
        self.far, self.near = far, near
        self.time = 0.0
        self.free = {"c": 0.0, "x": 0.0, "near": 0.0, "mid": 0.0}
        self.arrive = {}
        self.order = []

    def post(self, key, k, e):
        link = ("x" if e else "c", "near", "mid", "mid")[k]
        wire = {"c": 0.1, "x": 1.4, "near": 1.4, "mid": 2.8}[link] / PARTS
        self.free[link] = max(self.time, self.free[link]) + wire
        self.arrive[key] = self.free[link] + WAIT[link] + (0.7 if k and e else 0.0)

    def begin(self, name, h):
        for k in AHEAD:
            self.post((name, "z", h, k), k, 0)
        self.ahead(name, h, 0)
        for k in AHEAD:
            for e in range(1, self.near if (h, k) in DIRECT[name] else 1):
                self.post((name, "x", h, k, e), k, e)

    def ahead(self, name, h, k):
        for e in range(1, 1 if (h, k) in DIRECT[name] else self.near):
            self.post((name, "x", h, k, e), 0, e)
        self.post((name, "c", h, k, 0), 0, 0)

    def tasks(self):
        far, near, parts = range(self.far), range(self.near), range(PARTS)
        mixed = [("p2", h, k, e) for h in parts for k in far for e in near[1:]]
        out = []
        for h in parts:
            out += [((name, "far", h, k), [(name, "z", h, k)], 0.02)
                    for name in ("one", "two") for k in far[1:]]
        for h in parts:
            need = [("p1", h, 0, 0)] + [("p3", h, k) for k in far[1:]]
            need += [key for key in mixed if key[1] == h and (key[2] == 0 or (h, key[2]) in DIRECT["sum"])]
            out.append((("fresh", h), need, 0.35))
        for h in parts:
            for k in reversed(far[1:]):
                need = [("p1", h, k, 0)]
                need += [key for key in mixed if key[1:3] == (h, k) and (h, k) not in DIRECT["sum"]]
                out.append((("sum", h, k), need, 0.15))
        for h in parts:
            out += [(("mix", h, k, e), [("p1", h, k, e)], 0.14)
                    for k in reversed(far) for e in near[1:]]
        for h in parts:
            out += [((name, "near", h, k, e), [(name, "x", h, k, e)], 0.02)
                    for name in ("one", "two") for k in far for e in near[1:]]
        spread = [(h, k, e) for h in parts for e in reversed(near) for k in SPREAD]
        for name, side in (("first", "one"), ("second", "two")):
            out += [((name, u), [(side, "c", *u)], COST[name][0] / PARTS) for u in spread]
        return out

    def run(self, task):
        kind = task[0]
        if kind == "first":
            for unit in task[1:]:
                self.post(("p1", *unit), 0, 0)
        elif kind == "mix":
            h, k, e = task[1:]
            self.post(("p2", h, k, e), k if (h, k) in DIRECT["sum"] else 0, e)
        elif kind == "sum":
            self.post(("p3", *task[1:]), task[2], 0)
        elif kind == "fresh":
            self.begin("two", task[1])
        elif kind in ("one", "two") and task[1] == "far":
            self.ahead(kind, task[2], task[3])
        elif kind in ("one", "two"):
            self.post((kind, "c", *task[2:]), 0, 0)

    def build(self):
        for h in range(PARTS):
            self.begin("one", h)
        self.time = 0.5
        left = self.tasks()
        while left:
            known = [(max(self.arrive[n] for n in need), i) for i, (_, need, _) in enumerate(left)
                     if all(n in self.arrive for n in need)]
            ready = [i for when, i in known if when <= self.time]
            if not ready:
                self.time = min(when for when, _ in known)
                continue
            pick = min(ready)
            kind = left[pick][0][0]
            if kind in COST:
                alike = sorted((max(when, self.time), i) for when, i in known
                               if left[i][0][0] == kind and i != pick)
                if alike and alike[0][0] <= self.time + PAIR:
                    self.time = alike[0][0]
                    other = alike[0][1]
                    units = left[pick][0][1:] + left[other][0][1:]
                    for i in sorted((pick, other), reverse=True):
                        left.pop(i)
                    left.insert(0, ((kind, *units), [], COST[kind][1] / PARTS))
                    pick = 0
            task, _, cost = left.pop(pick)
            self.time += cost
            self.run(task)
            self.order.append(task)
        return self.order


def step_kernel(group, cells, blocks, brow_in, bcol_in, bcount_in, cell_in, gene_in, cell_new,
                gene_new, brow, bcol, bcount, held, spread, table, cell, gene, gene_bf, flipped, own_sum, parts, cell_bf,
                next_sum, next_parts, next_cell, numer, p1, p2, p3, t2, t3,
                p2m, p3m, t2m, t3m, acc, code, codem, other, otherm, group_sum, other_sum, size, even, *sems):
    spot = Spot(group)
    far, near, cores = spot.far, spot.near, spot.cores
    c = spot.c
    slots, width, _ = blocks.shape
    tiles = gene.shape[0]
    rows = cell.shape[0]
    prow = rows // PARTS
    sub = width // rows
    one_sems, two_sems = sems[0:4], [sems[4], *sems[1:4]]
    sent, r1, r2, r3, gr, nr, fr, orr, ls = sems[5:]
    s1, s2, u2, s3, u3, gs, ns, fs, uf, os = (sent.at[i] for i in range(10))
    greet("gene", group)
    greet("cell", cells)
    load_cell = pltpu.make_async_copy(cell_in, cell, ls.at[0])
    load_cell.start()
    small = [pltpu.make_async_copy(src, dst, ls.at[4 + i])
             for i, (src, dst) in enumerate(((brow_in, brow), (bcol_in, bcol), (bcount_in, bcount)))]
    for copy in small:
        copy.start()
    load_gene = pltpu.make_async_copy(gene_in, gene, ls.at[1])
    load_gene.start()
    load = pltpu.make_async_copy(blocks, held.at[pl.ds(0, slots)], ls.at[2])
    load.start()

    one = Gather(spot, cell_bf, prow, DIRECT["one"], one_sems)
    two = Gather(spot, next_cell, prow, DIRECT["two"], two_sems)
    load_cell.wait()
    for h in range(PARTS):
        one.place(h, 0, 0)[...] = cell[pl.ds(h * prow, prow), :].astype(BF)
    pl.semaphore_wait(pltpu.get_barrier_semaphore(), group - 1 + cells - 1)
    for h in range(PARTS):
        one.start(h)

    held[slots] = jnp.zeros((width, width), BF)
    for copy in small:
        copy.wait()
    lane = lax.broadcasted_iota(I32, (1, slots), 1)
    where = jnp.where(lane < bcount[0], brow[...] * tiles + bcol[...], -1)
    at = lax.broadcasted_iota(I32, (spread.shape[0], slots), 0)
    found = jnp.min(jnp.where(at == where, lane, slots), axis=1, keepdims=True)
    spread[...] = jnp.broadcast_to(found, spread.shape)
    load_table = pltpu.make_async_copy(spread, table, ls.at[3])
    load_table.start()

    def share(src, out, ss, sr):
        for d in range(1, group):
            send(src, out.at[spot.me], ss, sr.at[0], {"gene": lax.rem(spot.me + d, group)})

    load_gene.wait()
    first_sum = jnp.zeros((1, gene.shape[-1]), F32)
    for j in range(tiles):
        first_sum += jnp.sum(gene[j], axis=0, keepdims=True)
    own_sum[...] = first_sum
    parts[spot.me] = first_sum
    share(own_sum, parts, gs, gr)
    for j in range(tiles):
        gene_bf[j] = gene[j].astype(BF)
        flipped[j] = gene[j].astype(BF).T
        mean = jnp.mean(gene[j].astype(BF).astype(F32), axis=1, keepdims=True)
        even[j] = jnp.broadcast_to(mean, even.shape[1:])
    acc[...] = jnp.zeros_like(acc)
    load_table.wait()
    load.wait()

    def rows_of(source, units):
        return jnp.concatenate([source[h, spot.unit(k, e)] for h, k, e in units], axis=0)

    def ratio_of(rows_bf, units, j):
        found = []
        for h, k, e in units:
            for core in range(cores):
                g = spot.unit(k, e) * cores + core
                slot = table[(g // sub) * tiles + j, 0]
                if sub == 1:
                    found.append(held[slot, pl.ds(h * prow, prow), :])
                else:
                    first = pl.multiple_of(lax.rem(g, sub) * rows + h * prow, prow)
                    found.append(held[slot, pl.ds(first, prow), :])
        x = jnp.concatenate(found, axis=0)
        model = jnp.dot(rows_bf, flipped[j], preferred_element_type=F32)
        return (x.astype(F32) / model).astype(BF)

    c1 = {}
    mine_at = pl.ds(pl.multiple_of(c * prow, prow), prow)
    theirs_at = pl.ds(pl.multiple_of((1 - c) * prow, prow), prow)

    def first(*units):
        for unit in units:
            one.ready(*unit)
        rows_bf = rows_of(cell_bf, units)
        total = None
        for j in range(tiles):
            ratio = ratio_of(rows_bf, units, j)
            term = jnp.dot(ratio, gene_bf[j], preferred_element_type=F32)
            total = term if total is None else total + term
        for i, (h, k, e) in enumerate(units):
            u = spot.unit(k, e)
            numer[h, u] = total[i * cores * prow:(i + 1) * cores * prow]
            c1[h, k, e] = send(numer.at[h, u, theirs_at], p1.at[h, k, e], s1,
                               r1.at[h, k, e], spot.peer(0, 0, 1 - c))

    def weight(h, u):
        return jnp.mean(cell_bf[h, u, mine_at].astype(F32), axis=1, keepdims=True)

    def both(h, k, e):
        c1[h, k, e].wait_recv()
        u = spot.unit(k, e)
        return (numer[h, u, mine_at] + p1[h, k, e]) * weight(h, u)

    def mix(h, k, e):
        encode(both(h, k, e), t2.at[h, k, e], t2m.at[h, k, e])
        where = spot.peer(k if (h, k) in DIRECT["sum"] else 0, e, c)
        send(t2.at[h, k, e], p2.at[h, k, e], s2, r2.at[h, k, e - 1], where)
        send(t2m.at[h, k, e], p2m.at[h, k, e], u2, r2.at[h, k, e - 1], where)

    def summed(h, k, mixed):
        value = both(h, k, 0)
        for i in mixed:
            for e in range(1, near):
                drain(size.at[pl.ds(0, prow // 2 + 1)], r2.at[h, i, e - 1])
                value += decode(p2.at[h, i, e], p2m.at[h, i, e])
        return value

    def stage_sum(h, k):
        encode(summed(h, k, () if (h, k) in DIRECT["sum"] else (k,)), t3.at[h, k], t3m.at[h, k])
        where = spot.peer(k, 0, c)
        send(t3.at[h, k], p3.at[h, k], s3, r3.at[h, k - 1], where)
        send(t3m.at[h, k], p3m.at[h, k], u3, r3.at[h, k - 1], where)

    sums_of = {}

    def fresh(h):
        if "total" not in sums_of:
            drain(parts.at[pl.ds(0, group - 1)], gr.at[0])
            sums_of["total"] = jnp.sum(parts[...], axis=0)
        value = summed(h, 0, [k for k in range(far) if k == 0 or (h, k) in DIRECT["sum"]])
        for k in range(1, far):
            drain(size.at[pl.ds(0, prow // 2 + 1)], r3.at[h, k - 1])
            value += decode(p3.at[h, k], p3m.at[h, k])
        value = value / weight(h, spot.unit(0, 0))
        new = cell[pl.ds(h * prow, prow), :] * value / sums_of["total"]
        two.place(h, 0, 0)[...] = new.astype(BF)
        two.start(h)
        cell_new[pl.ds(h * prow, prow), :] = new
        sums_of[h] = jnp.sum(new, axis=0, keepdims=True)
        if all(i in sums_of for i in range(PARTS)):
            total = sums_of[0]
            for i in range(1, PARTS):
                total = total + sums_of[i]
            next_sum[...] = total
            next_parts[spot.me] = total
            share(next_sum, next_parts, ns, nr)

    def second(units, rows_bf, j):
        ratio = ratio_of(rows_bf, units, j)
        acc[j] += lax.dot_general(
            ratio, rows_bf, (((0,), (0,)), ((), ())), preferred_element_type=F32
        )

    order = Plan(far, near).build()
    late = [unit for task in order if task[0] == "second" for unit in task[1:]][-LAST:]
    for task in order:
        kind = task[0]
        if kind in ("one", "two"):
            side = one if kind == "one" else two
            if task[1] == "far":
                side.take_far(*task[2:])
            else:
                side.take_near(*task[2:])
        elif kind == "first":
            first(*task[1:])
        elif kind == "mix":
            mix(*task[1:])
        elif kind == "sum":
            stage_sum(*task[1:])
        elif kind == "fresh":
            fresh(*task[1:])
        else:
            units = [unit for unit in task[1:] if unit not in late]
            for unit in units:
                two.ready(*unit)
            rows_bf = rows_of(next_cell, units) if units else None
            for j in range(tiles if units else 0):
                second(units, rows_bf, j)
    for unit in late:
        two.ready(*unit)
    late_rows = rows_of(next_cell, late)

    def balance(j):
        return even[j]

    mine = lax.axis_index("cell")
    sum_copies = {}
    for j in range(tiles):
        second(late, late_rows, j)
        encode(acc[j] * balance(j), code.at[j], codem.at[j])
        for d in range(1, cells):
            where = {"cell": lax.rem(mine + d, cells)}
            send(code.at[j], other.at[mine, j], fs, fr.at[d - 1, j], where)
            send(codem.at[j], otherm.at[mine, j], uf, fr.at[d - 1, j], where)
        other[mine, j] = code[j]
        otherm[mine, j] = codem[j]
        if j == 0:
            drain(next_parts.at[pl.ds(0, group - 1)], nr.at[0])
            sums = jnp.sum(next_parts[...], axis=0)
            group_sum[...] = sums
            other_sum[mine] = sums
            for d in range(1, cells):
                sum_copies[d] = send(group_sum, other_sum.at[mine], os, orr.at[d - 1],
                                     {"cell": lax.rem(mine + d, cells)})
    for d in range(1, cells):
        sum_copies[d].wait_recv()
    sums = other_sum[0]
    for k in range(1, cells):
        sums += other_sum[k]
    for j in range(tiles):
        for d in range(1, cells):
            drain(size.at[pl.ds(0, width // 2 + 1)], fr.at[d - 1, j])
        value = decode(other.at[0, j], otherm.at[0, j])
        for k in range(1, cells):
            value += decode(other.at[k, j], otherm.at[k, j])
        gene_new[j] = gene[j] * (value / even[j]) / sums
    one.close()
    two.close()
    drain(numer.at[0], s1)
    drain(t2.at[:, :, 0:near - 1], s2)
    drain(t2m.at[:, :, 0:near - 1], u2)
    drain(t3.at[:, 1:far], s3)
    drain(t3m.at[:, 1:far], u3)
    drain(parts.at[pl.ds(0, group - 1)], gs)
    drain(next_parts.at[pl.ds(0, group - 1)], ns)
    drain(other.at[0:cells - 1], fs)
    drain(otherm.at[0:cells - 1], uf)
    drain(other_sum.at[0:cells - 1], os)


VMEM = pl.BlockSpec(memory_space=pltpu.VMEM)
HBM = pl.BlockSpec(memory_space=pltpu.HBM)


def step(group, cells, blocks, brow, bcol, bcount, cell, gene):
    far, near, cores = digits(group)
    slots, width, _ = blocks.shape
    tiles, _, rank = gene.shape
    rows = cell.shape[0]
    prow = rows // PARTS
    spots = rows * group // width * tiles
    dma = pltpu.SemaphoreType.DMA
    vmem = pltpu.VMEM
    hke = (PARTS, far, near)
    return pl.pallas_call(
        functools.partial(step_kernel, group, cells),
        out_shape=(vmem(cell.shape, F32), vmem(gene.shape, F32)),
        in_specs=[HBM] * 6,
        out_specs=(VMEM, VMEM),
        scratch_shapes=[
            vmem((1, slots), I32),
            vmem((1, slots), I32),
            pltpu.SMEM((1,), I32),
            vmem((slots + 1, width, width), BF),
            vmem((spots, 128), I32),
            pltpu.SMEM((spots, 128), I32),
            vmem((rows, rank), F32),
            vmem((tiles, width, rank), F32),
            vmem((tiles, width, rank), BF),
            vmem((tiles, rank, width), BF),
            vmem((1, rank), F32),
            vmem((group, 1, rank), F32),
            vmem((PARTS, far * near, cores * prow, rank), BF),
            vmem((1, rank), F32),
            vmem((group, 1, rank), F32),
            vmem((PARTS, far * near, cores * prow, rank), BF),
            vmem((PARTS, far * near, cores * prow, rank), F32),
            vmem((*hke, prow, rank), F32),
            vmem((*hke, prow, rank), I16),
            vmem((PARTS, far, prow, rank), I16),
            vmem((*hke, prow, rank), I16),
            vmem((PARTS, far, prow, rank), I16),
            vmem((*hke, 1, rank), F32),
            vmem((PARTS, far, 1, rank), F32),
            vmem((*hke, 1, rank), F32),
            vmem((PARTS, far, 1, rank), F32),
            vmem((tiles, width, rank), F32),
            vmem((tiles, width, rank), I16),
            vmem((tiles, 1, rank), F32),
            vmem((cells, tiles, width, rank), I16),
            vmem((cells, tiles, 1, rank), F32),
            vmem((1, rank), F32),
            vmem((cells, 1, rank), F32),
            vmem((width // 2 + 1, 1, rank), F32),
            vmem((tiles, width, rank), F32),
        ] + gather_sems(far, near) + [dma((3,)), dma((10,)), dma(hke)]
        + [dma((PARTS, far, near - 1)), dma((PARTS, far - 1))] + [dma((1,))] * 2
        + [dma((cells - 1, tiles)), dma((cells - 1,)), dma((7,))],
        compiler_params=pltpu.CompilerParams(
            collective_id=0, has_side_effects=True, vmem_limit_bytes=60 * 1024 * 1024
        ),
        name="update_step",
    )(blocks, brow, bcol, bcount, cell, gene)


def on_device(cells, group, blocks, brow, bcol, bcount, cell_factor, gene_factor):
    _, width, _ = blocks.shape
    rank = cell_factor.shape[-1]
    tiles = gene_factor.shape[0] // width
    cell_new, gene_new = step(group, cells, blocks, brow.reshape(1, -1), bcol.reshape(1, -1), bcount,
                              cell_factor, gene_factor.reshape(tiles, width, rank))
    return cell_new, gene_new.reshape(gene_factor.shape)


def solution(mesh):
    sizes = dict(mesh.shape)
    placed = (
        P(("cell", "gene"), None, None),
        P(("cell", "gene")),
        P(("cell", "gene")),
        P(("cell", "gene")),
        P(("cell", "gene"), None),
        P("gene", None),
    )
    return jax.shard_map(
        functools.partial(on_device, sizes["cell"], sizes["gene"]),
        mesh=mesh,
        in_specs=placed,
        out_specs=(P(("cell", "gene"), None), P("gene", None)),
        check_vma=False,
    )
```
